32 devices in a mesh: dp: 8 (over z, x), ctx: 4 (over y, core).
Axes of the slice: x: 2, y: 2, z: 4, core: 2. Of those that a mesh axis runs over, the one named last changes fastest.
Arguments:
- activations: bfloat16 [8, 512, 1024], P('dp', 'ctx'), may hold values from -6 to 6
- cotangent: bfloat16 [8, 512, 1024], P('dp', 'ctx'), may hold values from -6 to 6
- live_slots: int32 [8], P('dp'), may hold values 0 or 1
- doc_lengths: int32 [8, 4], P('dp'), may hold values from 1 to 320, 512 in all within a row
- inproj: float32 [1024, 3072], P(('dp', 'ctx')), may hold values from -0.1875 to 0.1875
- mom_inproj: float32 [1024, 3072], P(('dp', 'ctx')), may hold values from -4 to 4
- sqr_inproj: float32 [1024, 3072], P(('dp', 'ctx')), may hold values from 0.1 to 10
- gateproj: float32 [1024, 8], P(('dp', 'ctx')), may hold values from -0.1875 to 0.1875
- mom_gateproj: float32 [1024, 8], P(('dp', 'ctx')), may hold values from -4 to 4
- sqr_gateproj: float32 [1024, 8], P(('dp', 'ctx')), may hold values from 0.1 to 10
- outproj: float32 [1024, 1024], P(None, ('dp', 'ctx')), may hold values from -0.375 to 0.375
- mom_outproj: float32 [1024, 1024], P(None, ('dp', 'ctx')), may hold values from -4 to 4
- sqr_outproj: float32 [1024, 1024], P(None, ('dp', 'ctx')), may hold values from 0.1 to 10
- mlp_gate: float32 [1024, 2816], P(('dp', 'ctx')), may hold values from -0.1875 to 0.1875
- mom_mlp_gate: float32 [1024, 2816], P(('dp', 'ctx')), may hold values from -4 to 4
- sqr_mlp_gate: float32 [1024, 2816], P(('dp', 'ctx')), may hold values from 0.1 to 10
- mlp_up: float32 [1024, 2816], P(('dp', 'ctx')), may hold values from -0.1875 to 0.1875
- mom_mlp_up: float32 [1024, 2816], P(('dp', 'ctx')), may hold values from -4 to 4
- sqr_mlp_up: float32 [1024, 2816], P(('dp', 'ctx')), may hold values from 0.1 to 10
- mlp_down: float32 [2816, 1024], P(None, ('dp', 'ctx')), may hold values from -0.21875 to 0.21875
- mom_mlp_down: float32 [2816, 1024], P(None, ('dp', 'ctx')), may hold values from -4 to 4
- sqr_mlp_down: float32 [2816, 1024], P(None, ('dp', 'ctx')), may hold values from 0.1 to 10
- vectors: float32 [10240], P(('dp', 'ctx')), may hold values from 0.25 to 1.25
- mom_vectors: float32 [10240], P(('dp', 'ctx')), may hold values from -4 to 4
- sqr_vectors: float32 [10240], P(('dp', 'ctx')), may hold values from 0.1 to 10
- headvec: float32 [264], replicated, may hold values from -9 to 2, as said below
- mom_headvec: float32 [264], replicated, may hold values from -4 to 4
- sqr_headvec: float32 [264], replicated, may hold values from 0.1 to 10
Outputs:
- block_out: bfloat16 [8, 512, 1024], P('dp', 'ctx')
- input_grad: bfloat16 [8, 512, 1024], P('dp', 'ctx')
- grad_inproj: float32 [1024, 3072], P(('dp', 'ctx'))
- grad_gateproj: float32 [1024, 8], P(('dp', 'ctx'))
- grad_outproj: float32 [1024, 1024], P(None, ('dp', 'ctx'))
- grad_mlp_gate: float32 [1024, 2816], P(('dp', 'ctx'))
- grad_mlp_up: float32 [1024, 2816], P(('dp', 'ctx'))
- grad_mlp_down: float32 [2816, 1024], P(None, ('dp', 'ctx'))
- grad_vectors: float32 [10240], P(('dp', 'ctx'))
- grad_headvec: float32 [264], replicated
- new_inproj: float32 [1024, 3072], P(('dp', 'ctx'))
- newmom_inproj: float32 [1024, 3072], P(('dp', 'ctx'))
- newsqr_inproj: float32 [1024, 3072], P(('dp', 'ctx'))
- new_gateproj: float32 [1024, 8], P(('dp', 'ctx'))
- newmom_gateproj: float32 [1024, 8], P(('dp', 'ctx'))
- newsqr_gateproj: float32 [1024, 8], P(('dp', 'ctx'))
- new_outproj: float32 [1024, 1024], P(None, ('dp', 'ctx'))
- newmom_outproj: float32 [1024, 1024], P(None, ('dp', 'ctx'))
- newsqr_outproj: float32 [1024, 1024], P(None, ('dp', 'ctx'))
- new_mlp_gate: float32 [1024, 2816], P(('dp', 'ctx'))
- newmom_mlp_gate: float32 [1024, 2816], P(('dp', 'ctx'))
- newsqr_mlp_gate: float32 [1024, 2816], P(('dp', 'ctx'))
- new_mlp_up: float32 [1024, 2816], P(('dp', 'ctx'))
- newmom_mlp_up: float32 [1024, 2816], P(('dp', 'ctx'))
- newsqr_mlp_up: float32 [1024, 2816], P(('dp', 'ctx'))
- new_mlp_down: float32 [2816, 1024], P(None, ('dp', 'ctx'))
- newmom_mlp_down: float32 [2816, 1024], P(None, ('dp', 'ctx'))
- newsqr_mlp_down: float32 [2816, 1024], P(None, ('dp', 'ctx'))
- new_vectors: float32 [10240], P(('dp', 'ctx'))
- newmom_vectors: float32 [10240], P(('dp', 'ctx'))
- newsqr_vectors: float32 [10240], P(('dp', 'ctx'))
- new_headvec: float32 [264], replicated
- newmom_headvec: float32 [264], replicated
- newsqr_headvec: float32 [264], replicated
The draws below stay inside these ranges and needn't reach their ends.
Inputs may be any that keep to these rules, and one draw needn't show every extreme that they name: `doc_lengths`: each row holds 4 document lengths summing to 512, the largest exactly 320. `headvec`: gains in the first 256 entries, then 4 log scales, then 4 offsets.
All inputs are finite; a program needn't handle non-finite values. No bound on the sum of `live_slots` on one device may be relied on, other than what follows from the above.
Results may differ from the reference program's by a relative error of at most 0.014.
The reference program's roundings to bfloat16 on the way (of `normed`, `mixed`, `normed_two`, `hidden` and `g_branch`) count: a program that leaves them out, or rounds other values in their place, can miss the bound.
Values may be sent and summed in bfloat16 or wider, within the bound.
No kernel may reach another device: no remote copies, remote signals or barrier semaphores. Data moves between devices by JAX's collectives and lax.ppermute only.
A program may use at most 256 MiB of HBM per device.

```python
import math
import jax
import jax.numpy as jnp
import numpy as np
from jax import lax

D = 1024
H = 4
DK = 128
DV = 256
FF = 2816
CONV = 4
GROUP = 64
DOCS = 4
STEP = 5
CONVC = 2048
QKVG = 3072
SEQ = 512
BATCH = 8
MOST_DOC = 320
VEC = 10240
SMALL = 264


def draw_headvec(key, part):
    subkeys = jax.random.split(jax.random.fold_in(key, 11), 3)
    head_gains = jax.random.uniform(subkeys[0], (DV,), jnp.float32, 0.5, 1.5)
    log_scales = jax.random.uniform(subkeys[1], (H,), jnp.float32, -2.0, 2.0)
    offsets = jax.random.uniform(subkeys[2], (H,), jnp.float32, -9.0, -3.0)
    return jnp.concatenate([head_gains, log_scales, offsets]).astype(jnp.float32)


def set_ends(values, own_key, smallest, high):
    place = [jax.random.randint(jax.random.fold_in(own_key, axis), (), 0, length) for axis, length in enumerate(values.shape)]
    widest = values.shape.index(max(values.shape))
    beside = place[:widest] + [(place[widest] + 1) % values.shape[widest]] + place[widest + 1:]
    return values.at[tuple(place)].set(smallest).at[tuple(beside)].set(high)


def level_of(stream_key, shape, shards, smallest, top_value):
    def one(axis_at, blocks):
        heights = jax.random.uniform(jax.random.fold_in(jax.random.fold_in(stream_key, 6), axis_at), (blocks,), jnp.float32, smallest / len(shards), top_value / len(shards))
        return jnp.repeat(jnp.exp(heights), shape[axis_at] // blocks).reshape((-1,) + (1,) * (len(shape) - axis_at - 1))

    level = one(*shards[0])
    for cut in shards[1:]:
        level = level * one(*cut)
    return level


def profile(number_of, total, limit, slope):
    portions = [(1 << 20) // math.isqrt(grade ** slope) + 1 for grade in range(2, number_of + 1)]
    surplus, counts = total - limit - (number_of - 1), [1] * (number_of - 1)
    while surplus > 0:
        free = [i for i in range(number_of - 1) if counts[i] < limit]
        pool, remaining = sum([portions[i] for i in free]), surplus
        for i in free:
            addition = min(limit - counts[i], max(1, remaining * portions[i] // pool), surplus)
            counts[i] = counts[i] + addition
            surplus = surplus - addition
    return np.array([limit] + counts)


def ragged_sizes(own_key, amount, total, bound, skew):
    if amount == 2:
        one = jax.random.randint(own_key, (), max(1, total - bound), min(bound, total - 1) + 1)
        return jnp.stack([one, total - one])
    sizes = jnp.asarray(profile(amount, total, bound, skew), jnp.int32)
    couples = (amount - 1) // 2
    donor, receiver = sizes[1:1 + 2 * couples:2], sizes[2:2 + 2 * couples:2]
    room = jnp.minimum(donor - 1, bound - receiver)
    shifted = jax.random.randint(jax.random.fold_in(own_key, 1), (couples,), 0, 1 << 20) % (room + 1)
    sizes = sizes.at[1:1 + 2 * couples:2].set(donor - shifted).at[2:2 + 2 * couples:2].set(receiver + shifted)
    return sizes[jax.random.permutation(jax.random.fold_in(own_key, 2), amount)]


def noise(stream_key, dims, scale, bound, cuts=(), kind=jnp.bfloat16):
    values = jax.random.normal(stream_key, dims, jnp.float32) * scale
    if len(cuts) > 0:
        values = level_of(stream_key, dims, cuts, -0.22, 0.18) * values
    return jnp.clip(values, min=-bound, max=bound).astype(kind)


def setup_inputs(seed: int = 0) -> dict:
    streams_of = jax.random.split(jax.random.key(seed), 29)
    activations = noise(streams_of[0], (BATCH, SEQ, D), 1.0, 6.0, ((0, 8), (1, 4)))
    cotangent = noise(streams_of[1], (BATCH, SEQ, D), 1.0, 6.0, ((0, 8), (1, 4)))
    live_slots = set_ends((jax.random.randint(streams_of[2], (BATCH,), 0, 4) < 3).astype(jnp.int32), jax.random.fold_in(streams_of[2], 1), 0, 1)
    doc_lengths = jax.vmap(lambda own: ragged_sizes(own, DOCS, SEQ, MOST_DOC, 0))(jax.random.split(streams_of[3], BATCH)).reshape((BATCH, DOCS)).astype(jnp.int32)
    inproj = noise(streams_of[4], (D, QKVG), D ** -0.5, 0.1875, ((0, 32),), jnp.float32)
    mom_inproj = noise(streams_of[5], (D, QKVG), 1.0, 4.0, ((0, 32),), jnp.float32)
    sqr_inproj = jnp.clip(jnp.exp(math.log(10.0) - 4.6051702 * jax.random.uniform(streams_of[6], (D, QKVG), jnp.float32) ** level_of(streams_of[6], (D, QKVG), ((0, 32),), -0.2, 0.2)), 0.1, 10.0)
    gateproj = noise(streams_of[7], (D, 2 * H), D ** -0.5, 0.1875, ((0, 32),), jnp.float32)
    mom_gateproj = noise(streams_of[8], (D, 2 * H), 1.0, 4.0, ((0, 32),), jnp.float32)
    sqr_gateproj = jnp.clip(jnp.exp(math.log(10.0) - 4.6051702 * jax.random.uniform(streams_of[9], (D, 2 * H), jnp.float32) ** level_of(streams_of[9], (D, 2 * H), ((0, 32),), -0.2, 0.2)), 0.1, 10.0)
    outproj = noise(streams_of[10], (H * DV, D), (H * DV // 4) ** -0.5, 0.375, ((1, 32),), jnp.float32)
    mom_outproj = noise(streams_of[11], (H * DV, D), 1.0, 4.0, ((1, 32),), jnp.float32)
    sqr_outproj = jnp.clip(jnp.exp(math.log(10.0) - 4.6051702 * jax.random.uniform(streams_of[12], (H * DV, D), jnp.float32) ** level_of(streams_of[12], (H * DV, D), ((1, 32),), -0.2, 0.2)), 0.1, 10.0)
    mlp_gate = noise(streams_of[13], (D, FF), D ** -0.5, 0.1875, ((0, 32),), jnp.float32)
    mom_mlp_gate = noise(streams_of[14], (D, FF), 1.0, 4.0, ((0, 32),), jnp.float32)
    sqr_mlp_gate = jnp.clip(jnp.exp(math.log(10.0) - 4.6051702 * jax.random.uniform(streams_of[15], (D, FF), jnp.float32) ** level_of(streams_of[15], (D, FF), ((0, 32),), -0.2, 0.2)), 0.1, 10.0)
    mlp_up = noise(streams_of[16], (D, FF), D ** -0.5, 0.1875, ((0, 32),), jnp.float32)
    mom_mlp_up = noise(streams_of[17], (D, FF), 1.0, 4.0, ((0, 32),), jnp.float32)
    sqr_mlp_up = jnp.clip(jnp.exp(math.log(10.0) - 4.6051702 * jax.random.uniform(streams_of[18], (D, FF), jnp.float32) ** level_of(streams_of[18], (D, FF), ((0, 32),), -0.2, 0.2)), 0.1, 10.0)
    mlp_down = noise(streams_of[19], (FF, D), (FF // 4) ** -0.5, 0.21875, ((1, 32),), jnp.float32)
    mom_mlp_down = noise(streams_of[20], (FF, D), 1.0, 4.0, ((1, 32),), jnp.float32)
    sqr_mlp_down = jnp.clip(jnp.exp(math.log(10.0) - 4.6051702 * jax.random.uniform(streams_of[21], (FF, D), jnp.float32) ** level_of(streams_of[21], (FF, D), ((1, 32),), -0.2, 0.2)), 0.1, 10.0)
    vectors = jnp.clip(0.25 + 1.0 * jax.random.uniform(streams_of[22], (VEC,), jnp.float32) ** level_of(streams_of[22], (VEC,), ((0, 32),), -0.2, 0.2), 0.25, 1.25)
    mom_vectors = noise(streams_of[23], (VEC,), 1.0, 4.0, ((0, 32),), jnp.float32)
    sqr_vectors = jnp.clip(jnp.exp(math.log(10.0) - 4.6051702 * jax.random.uniform(streams_of[24], (VEC,), jnp.float32) ** level_of(streams_of[24], (VEC,), ((0, 32),), -0.2, 0.2)), 0.1, 10.0)
    headvec = draw_headvec(jax.random.fold_in(streams_of[28], 71), 0)
    mom_headvec = noise(streams_of[26], (SMALL,), 1.0, 4.0, (), jnp.float32)
    sqr_headvec = jnp.clip(jnp.exp(jax.random.uniform(streams_of[27], (SMALL,), jnp.float32, math.log(0.1), math.log(10.0))), 0.1, 10.0)
    return dict(activations=activations, cotangent=cotangent, live_slots=live_slots, doc_lengths=doc_lengths, inproj=inproj, mom_inproj=mom_inproj, sqr_inproj=sqr_inproj, gateproj=gateproj, mom_gateproj=mom_gateproj, sqr_gateproj=sqr_gateproj, outproj=outproj, mom_outproj=mom_outproj, sqr_outproj=sqr_outproj, mlp_gate=mlp_gate, mom_mlp_gate=mom_mlp_gate, sqr_mlp_gate=sqr_mlp_gate, mlp_up=mlp_up, mom_mlp_up=mom_mlp_up, sqr_mlp_up=sqr_mlp_up, mlp_down=mlp_down, mom_mlp_down=mom_mlp_down, sqr_mlp_down=sqr_mlp_down, vectors=vectors, mom_vectors=mom_vectors, sqr_vectors=sqr_vectors, headvec=headvec, mom_headvec=mom_headvec, sqr_headvec=sqr_headvec)


NORM_EPS = 1e-06
exact_mode = lax.Precision.HIGHEST
beta_one = 0.9
beta_two = 0.999
learn_rate = 0.01
weight_decay = 0.1
adam_eps = 1e-08

def doc_positions(lengths, first, count):
    ends = jnp.cumsum(lengths, axis=-1).astype(jnp.int32)
    starts = (ends - lengths).astype(jnp.int32)
    places = (first + jnp.arange(count, dtype=jnp.int32)).astype(jnp.int32)
    owner = lax.optimization_barrier(jnp.max(jnp.where(starts[:, None, :] <= places[None, :, None], starts[:, None, :], 0), axis=-1))
    return (places[None, :] - owner).astype(jnp.int32)

def group_step(state, queries, keys_in, values, betas, log_decay, positions):
    width = queries.shape[2]
    cumul = jnp.cumsum(log_decay, axis=-1)
    order_index = jnp.arange(width, dtype=jnp.int32)
    distance = order_index[:, None] - order_index[None, :]
    same_doc = (distance >= 0)[None, None] & (positions[:, None, :, None] >= distance[None, None])
    decays = jnp.exp(jnp.minimum(cumul[..., :, None] - cumul[..., None, :], 0.0)) * same_doc.astype(jnp.float32)
    carried = jnp.exp(cumul) * (positions[:, None, :] >= order_index[None, None, :] + 1).astype(jnp.float32)
    key_dots = jnp.einsum('shtk,shik->shti', keys_in, keys_in, precision=exact_mode)
    lower = betas[..., :, None] * decays * key_dots * (distance > 0).astype(jnp.float32)
    key_state = jnp.einsum('shtk,shvk->shtv', keys_in, state, precision=exact_mode)
    targets = betas[..., None] * values - (betas * carried)[..., None] * key_state
    written = jax.scipy.linalg.solve_triangular(jnp.eye(width, dtype=jnp.float32) + lower, targets, lower=True, unit_diagonal=True)
    query_dots = jnp.einsum('shtk,shik->shti', queries, keys_in, precision=exact_mode)
    query_state = jnp.einsum('shtk,shvk->shtv', queries, state, precision=exact_mode)
    outputs = carried[..., None] * query_state + jnp.einsum('shti,shiv->shtv', decays * query_dots, written, precision=exact_mode)
    final_row = decays[..., width - 1, :]
    new_state = carried[..., width - 1][..., None, None] * state + jnp.einsum('shiv,shik->shvk', written, final_row[..., None] * keys_in, precision=exact_mode)
    return (new_state, outputs)

def pre_core(proj_ext, beta_decay, conv_taps, log_scale, offsets, positions):
    slots, length = positions.shape
    convolved = jnp.zeros((slots, length, proj_ext.shape[2]), jnp.float32)
    for tap in range(CONV):
        valid = (positions >= CONV - 1 - tap).astype(jnp.float32)[..., None]
        convolved = convolved + conv_taps[tap] * proj_ext[:, tap:tap + length, :] * valid
    acts = jax.nn.silu(convolved)
    width_q = H * DK
    queries = acts[..., :width_q].reshape(slots, length, H, DK)
    keys_in = acts[..., width_q:2 * width_q].reshape(slots, length, H, DK)
    values = acts[..., 2 * width_q:].reshape(slots, length, H, DV)
    queries = queries * lax.rsqrt(lax.optimization_barrier(jnp.sum(queries * queries, -1, keepdims=True)) + NORM_EPS) * DK ** (-0.5)
    keys_in = keys_in * lax.rsqrt(lax.optimization_barrier(jnp.sum(keys_in * keys_in, -1, keepdims=True)) + NORM_EPS)
    betas = jax.nn.sigmoid(beta_decay[..., :H])
    log_decay = -jnp.exp(log_scale) * jax.nn.softplus(beta_decay[..., H:] + offsets)
    queries = jnp.transpose(queries, (0, 2, 1, 3))
    keys_in = jnp.transpose(keys_in, (0, 2, 1, 3))
    values = jnp.transpose(values, (0, 2, 1, 3))
    betas = jnp.transpose(betas, (0, 2, 1))
    log_decay = jnp.transpose(log_decay, (0, 2, 1))
    values_aug = jnp.concatenate([values, jnp.zeros((slots, H, length, DK), jnp.float32)], axis=-1)
    ident = jnp.broadcast_to(jnp.eye(DK, dtype=jnp.float32), (slots, H, DK, DK))
    state = jnp.concatenate([jnp.zeros((slots, H, DV, DK), jnp.float32), ident], axis=2)
    pieces = []
    for offset in range(0, length, GROUP):
        part = slice(offset, offset + GROUP)
        state, outputs = group_step(state, queries[:, :, part], keys_in[:, :, part], values_aug[:, :, part], betas[:, :, part], log_decay[:, :, part], positions[:, part])
        pieces.append(outputs)
    outs_all = jnp.concatenate(pieces, axis=2)
    return (state[:, :, DV:, :], state[:, :, :DV, :], outs_all[..., :DV], outs_all[..., DV:])

def post_core(local_out, query_mix, state_in, gate, head_gain):
    slots, heads, length, _ = local_out.shape
    full = local_out + jnp.einsum('shtk,shvk->shtv', query_mix, state_in, precision=exact_mode)
    full = full * lax.rsqrt(lax.optimization_barrier(jnp.mean(full * full, -1, keepdims=True)) + NORM_EPS) * head_gain
    full = jnp.transpose(full, (0, 2, 1, 3)).reshape(slots, length, heads * DV)
    return full * jax.nn.silu(gate)

def adamw(weights, moment, square, grads):
    new_moment = beta_one * moment + (1.0 - beta_one) * grads
    new_square = beta_two * square + (1.0 - beta_two) * grads * grads
    corrected = new_moment / (1.0 - beta_one ** STEP)
    scaled = new_square / (1.0 - beta_two ** STEP)
    new_weights = weights - learn_rate * (corrected / (jnp.sqrt(scaled) + adam_eps) + weight_decay * weights)
    return (new_weights, new_moment, new_square)

def reference(activations, cotangent, live_slots, doc_lengths, inproj, mom_inproj, sqr_inproj, gateproj, mom_gateproj, sqr_gateproj, outproj, mom_outproj, sqr_outproj, mlp_gate, mom_mlp_gate, sqr_mlp_gate, mlp_up, mom_mlp_up, sqr_mlp_up, mlp_down, mom_mlp_down, sqr_mlp_down, vectors, mom_vectors, sqr_vectors, headvec, mom_headvec, sqr_headvec):
    full_in = inproj.astype(jnp.bfloat16)
    full_ab = gateproj.astype(jnp.bfloat16)
    full_out = outproj.astype(jnp.bfloat16)
    full_wg = mlp_gate.astype(jnp.bfloat16)
    full_wu = mlp_up.astype(jnp.bfloat16)
    full_wd = mlp_down.astype(jnp.bfloat16)
    vec_used = vectors.astype(jnp.bfloat16).astype(jnp.float32)
    norm_gain = vec_used[:D]
    conv_taps = vec_used[D:D + CONV * CONVC].reshape(CONV, CONVC)
    mlp_gain = vec_used[D + CONV * CONVC:]
    head_gain = headvec[:DV]
    log_scale = headvec[DV:DV + H]
    offsets = headvec[DV + H:]
    block = math.gcd(BATCH, max(1, 4096 // SEQ))
    nblocks = BATCH // block

    def one_block(carry, pieces):
        inputs, grads_in, lives, lengths = pieces
        count = inputs.shape[0]
        xfull = inputs.astype(jnp.float32)
        inv_rms = lax.rsqrt(lax.optimization_barrier(jnp.mean(xfull * xfull, -1, keepdims=True)) + NORM_EPS)
        unit = xfull * inv_rms
        normed = (unit * norm_gain).astype(jnp.bfloat16)
        flat = normed.reshape(-1, D)
        proj = jnp.dot(flat.astype(jnp.float32), full_in.astype(jnp.float32), preferred_element_type=jnp.float32).reshape(count, SEQ, QKVG)
        beta_decay = jnp.dot(flat.astype(jnp.float32), full_ab.astype(jnp.float32), preferred_element_type=jnp.float32).reshape(count, SEQ, 2 * H)
        positions = doc_positions(lengths, 0, SEQ)
        proj_ext = jnp.pad(proj[..., :CONVC], ((0, 0), (CONV - 1, 0), (0, 0)))
        gate = proj[..., CONVC:]

        def mixer(ext_in, bd_in, gate_in, taps_in, scale_in, offs_in, hgain_in):
            p_mat, u_mat, local_out, query_mix = pre_core(ext_in, bd_in, taps_in, scale_in, offs_in, positions)
            return post_core(local_out, query_mix, jnp.zeros_like(u_mat), gate_in, hgain_in)
        mixed_f, backward = jax.vjp(mixer, proj_ext, beta_decay, gate, conv_taps, log_scale, offsets, head_gain)
        mixed = mixed_f.astype(jnp.bfloat16)
        mixed_flat = mixed.reshape(-1, H * DV)
        branch = jnp.dot(mixed_flat.astype(jnp.float32), full_out.astype(jnp.float32), preferred_element_type=jnp.float32).reshape(count, SEQ, D)
        live_f = lives.astype(jnp.float32)[:, None, None]
        resid = xfull + live_f * branch
        inv_two = lax.rsqrt(lax.optimization_barrier(jnp.mean(resid * resid, -1, keepdims=True)) + NORM_EPS)
        unit_two = resid * inv_two
        normed_two = (unit_two * mlp_gain).astype(jnp.bfloat16).reshape(-1, D)
        hgate = jnp.dot(normed_two.astype(jnp.float32), full_wg.astype(jnp.float32), preferred_element_type=jnp.float32)
        hup = jnp.dot(normed_two.astype(jnp.float32), full_wu.astype(jnp.float32), preferred_element_type=jnp.float32)
        sigma = jax.nn.sigmoid(hgate)
        silu_gate = hgate * sigma
        hidden = (silu_gate * hup).astype(jnp.bfloat16)
        mlp_out = jnp.dot(hidden.astype(jnp.float32), full_wd.astype(jnp.float32), preferred_element_type=jnp.float32).reshape(count, SEQ, D)
        out_block = (resid + live_f * mlp_out).astype(jnp.bfloat16)
        cot_f = grads_in.astype(jnp.float32)
        g_mlp = (cot_f * live_f).astype(jnp.bfloat16).reshape(-1, D)
        d_hidden = jnp.dot(g_mlp.astype(jnp.float32), full_wd.T.astype(jnp.float32), preferred_element_type=jnp.float32)
        g_wd = jnp.dot(hidden.T.astype(jnp.float32), g_mlp.astype(jnp.float32), preferred_element_type=jnp.float32)
        d_hgate = (d_hidden * hup * sigma * (1.0 + hgate * (1.0 - sigma))).astype(jnp.bfloat16)
        d_hup = (d_hidden * silu_gate).astype(jnp.bfloat16)
        g_wg = jnp.dot(normed_two.T.astype(jnp.float32), d_hgate.astype(jnp.float32), preferred_element_type=jnp.float32)
        g_wu = jnp.dot(normed_two.T.astype(jnp.float32), d_hup.astype(jnp.float32), preferred_element_type=jnp.float32)
        d_normed_two = (jnp.dot(d_hgate.astype(jnp.float32), full_wg.T.astype(jnp.float32), preferred_element_type=jnp.float32) + jnp.dot(d_hup.astype(jnp.float32), full_wu.T.astype(jnp.float32), preferred_element_type=jnp.float32)).reshape(count, SEQ, D)
        d_gain_two = lax.optimization_barrier(jnp.sum(d_normed_two * unit_two, axis=(0, 1)))
        d_unit_two = d_normed_two * mlp_gain
        d_resid = cot_f + inv_two * (d_unit_two - unit_two * lax.optimization_barrier(jnp.mean(d_unit_two * unit_two, -1, keepdims=True)))
        g_branch = (d_resid * live_f).astype(jnp.bfloat16)
        g_flat = g_branch.reshape(-1, D)
        d_mixed = jnp.dot(g_flat.astype(jnp.float32), full_out.T.astype(jnp.float32), preferred_element_type=jnp.float32).reshape(count, SEQ, H * DV)
        g_out = jnp.dot(mixed_flat.T.astype(jnp.float32), g_flat.astype(jnp.float32), preferred_element_type=jnp.float32)
        d_ext, d_bd, d_gate, d_taps, d_scale, d_offs, d_hgain = backward(d_mixed)
        d_proj = jnp.concatenate([d_ext[:, CONV - 1:, :], d_gate], axis=-1).astype(jnp.bfloat16).reshape(-1, QKVG)
        d_bd_b = d_bd.astype(jnp.bfloat16).reshape(-1, 2 * H)
        g_in = jnp.dot(flat.T.astype(jnp.float32), d_proj.astype(jnp.float32), preferred_element_type=jnp.float32)
        g_ab = jnp.dot(flat.T.astype(jnp.float32), d_bd_b.astype(jnp.float32), preferred_element_type=jnp.float32)
        d_normed = jnp.dot(d_proj.astype(jnp.float32), full_in.T.astype(jnp.float32), preferred_element_type=jnp.float32) + jnp.dot(d_bd_b.astype(jnp.float32), full_ab.T.astype(jnp.float32), preferred_element_type=jnp.float32)
        d_normed = d_normed.reshape(count, SEQ, D)
        d_gain = lax.optimization_barrier(jnp.sum(d_normed * unit, axis=(0, 1)))
        d_unit = d_normed * norm_gain
        d_input = (d_resid + inv_rms * (d_unit - unit * lax.optimization_barrier(jnp.mean(d_unit * unit, -1, keepdims=True)))).astype(jnp.bfloat16)
        g_vec = jnp.concatenate([d_gain, d_taps.reshape(-1), d_gain_two])
        g_small = jnp.concatenate([d_hgain, d_scale, d_offs])
        totals = (carry[0] + g_in, carry[1] + g_ab, carry[2] + g_out, carry[3] + g_wg, carry[4] + g_wu, carry[5] + g_wd, carry[6] + g_vec, carry[7] + g_small)
        return (totals, (out_block, d_input))
    init = (jnp.zeros((D, QKVG), jnp.float32), jnp.zeros((D, 2 * H), jnp.float32), jnp.zeros((H * DV, D), jnp.float32), jnp.zeros((D, FF), jnp.float32), jnp.zeros((D, FF), jnp.float32), jnp.zeros((FF, D), jnp.float32), jnp.zeros((VEC,), jnp.float32), jnp.zeros((SMALL,), jnp.float32))
    stacked = (activations.reshape(nblocks, block, SEQ, D), cotangent.reshape(nblocks, block, SEQ, D), live_slots.reshape(nblocks, block), doc_lengths.reshape(nblocks, block, DOCS))
    totals, (outs, dins) = lax.scan(one_block, init, stacked)
    block_out = outs.reshape(BATCH, SEQ, D)
    input_grad = dins.reshape(BATCH, SEQ, D)
    g_in, g_ab, g_out, g_wg, g_wu, g_wd, g_vec, g_small = totals
    n_in, nm_in, ns_in = adamw(inproj, mom_inproj, sqr_inproj, g_in)
    n_ab, nm_ab, ns_ab = adamw(gateproj, mom_gateproj, sqr_gateproj, g_ab)
    n_out, nm_out, ns_out = adamw(outproj, mom_outproj, sqr_outproj, g_out)
    n_wg, nm_wg, ns_wg = adamw(mlp_gate, mom_mlp_gate, sqr_mlp_gate, g_wg)
    n_wu, nm_wu, ns_wu = adamw(mlp_up, mom_mlp_up, sqr_mlp_up, g_wu)
    n_wd, nm_wd, ns_wd = adamw(mlp_down, mom_mlp_down, sqr_mlp_down, g_wd)
    n_vec, nm_vec, ns_vec = adamw(vectors, mom_vectors, sqr_vectors, g_vec)
    n_small, nm_small, ns_small = adamw(headvec, mom_headvec, sqr_headvec, g_small)
    return (block_out, input_grad, g_in, g_ab, g_out, g_wg, g_wu, g_wd, g_vec, g_small, n_in, nm_in, ns_in, n_ab, nm_ab, ns_ab, n_out, nm_out, ns_out, n_wg, nm_wg, ns_wg, n_wu, nm_wu, ns_wu, n_wd, nm_wd, ns_wd, n_vec, nm_vec, ns_vec, n_small, nm_small, ns_small)
```

```python
import jax
import jax.numpy as jnp
from jax import lax
from jax.experimental import pallas as pl
from jax.experimental.pallas import tpu as pltpu
from jax.sharding import PartitionSpec as P

D = 1024
H = 4
DK = 128
DV = 256
CONV = 4
GROUP = 64
STEP = 5
CONVC = 2048

NORM_EPS = 1e-06
beta_one = 0.9
beta_two = 0.999
learn_rate = 0.01
weight_decay = 0.1
adam_eps = 1e-08

F32 = jnp.float32
BF = jnp.bfloat16
EXACT = lax.Precision.HIGHEST

HEADQ = DK
HEADC = 2 * DK + DV
HEADG = HEADC + DV
EXTRA = 128


def mm(a, b, lhs=1, rhs=0):
    return lax.dot_general(
        a, b, (((lhs,), (rhs,)), ((), ())), precision=EXACT, preferred_element_type=F32
    )


def shift_rows(value, steps):
    return pltpu.roll(value, steps % value.shape[0], axis=0)


def pre_stage(px_ref, taps_ref, par_ref, pos_ref):
    rows = px_ref.shape[0]
    pos = pos_ref[...]
    x = px_ref[:, :HEADC]
    conv = x * taps_ref[CONV - 1 : CONV, :]
    for s in range(1, CONV):
        valid = (pos >= s).astype(F32)
        conv = conv + taps_ref[CONV - 1 - s : CONV - s, :] * (shift_rows(x, s) * valid)
    sig = jax.nn.sigmoid(conv)
    act = conv * sig
    qr = act[:, :DK]
    kr = act[:, DK : 2 * DK]
    v = act[:, 2 * DK :]
    rq = lax.rsqrt(jnp.sum(qr * qr, -1, keepdims=True) + NORM_EPS)
    rk = lax.rsqrt(jnp.sum(kr * kr, -1, keepdims=True) + NORM_EPS)
    q = qr * rq * DK ** (-0.5)
    k = kr * rk
    mix = px_ref[:, HEADG : HEADG + EXTRA]
    lane = lax.broadcasted_iota(jnp.int32, (rows, EXTRA), 1)
    b_raw = jnp.sum(jnp.where(lane == 0, mix, 0.0), -1, keepdims=True)
    a_raw = jnp.sum(jnp.where(lane == 1, mix, 0.0), -1, keepdims=True)
    beta = jax.nn.sigmoid(b_raw)
    scale = -jnp.exp(jnp.zeros((rows, 1), F32) + par_ref[0])
    shifted = a_raw + par_ref[1]
    soft = jnp.maximum(shifted, 0.0) + jnp.log1p(jnp.exp(-jnp.abs(shifted)))
    logd = scale * soft
    return pos, x, conv, sig, qr, kr, rq, rk, q, k, v, beta, scale, shifted, logd


def block_masks(width):
    row = lax.broadcasted_iota(jnp.int32, (width, width), 0)
    col = lax.broadcasted_iota(jnp.int32, (width, width), 1)
    same = (row // GROUP) == (col // GROUP)
    return row, col, same


def gates_of(pos, logd, width):
    row, col, same = block_masks(width)
    lower = ((row >= col) & same).astype(F32)
    lb = jnp.broadcast_to(logd, (width, width))
    cum_t = mm(lower, lb)
    cum_i = mm(lb, lower, 0, 1)
    keep = ((row >= col) & same & (pos >= row - col)).astype(F32)
    decays = jnp.exp(jnp.minimum(cum_t - cum_i, 0.0)) * keep
    at = lax.broadcasted_iota(jnp.int32, (width, 1), 0) % GROUP
    carried = jnp.exp(cum_t[:, :1]) * (pos >= at + 1).astype(F32)
    strict = (row > col).astype(F32)
    return decays, carried, lower, strict


def unit_inverse(low):
    width = low.shape[0]
    row, col, same = block_masks(width)
    size = 1
    out = None
    while size < GROUP:
        join = (
            ((row // (2 * size)) == (col // (2 * size)))
            & ((row // size) % 2 == 1)
            & ((col // size) % 2 == 0)
        )
        part = jnp.where(join, low, 0.0)
        if out is None:
            out = (row == col).astype(F32) - part
        else:
            out = out - mm(mm(out, part), out)
        size *= 2
    return out


def final_of(decays, width):
    row, col, same = block_masks(width)
    last = ((col % GROUP) == GROUP - 1) & same
    pick = jnp.where((row % GROUP) == GROUP - 1, decays, 0.0)
    ones = jnp.ones((width, DK), F32)
    return mm(pick, ones, 0, 0)


def core_fwd_kernel(
    px_ref, taps_ref, par_ref, pos_ref, hg_ref,
    mixed_ref, state_ref, inv_ref, wr_ref, y_ref, qt_ref, m_ref, o_ref,
    n_ref,
):
    rows = px_ref.shape[0]
    width = min(4 * GROUP, rows)
    pos, x, conv, sig, qr, kr, rq, rk, q, k, v, beta, scale, shifted, logd = pre_stage(
        px_ref, taps_ref, par_ref, pos_ref
    )
    spans = [slice(i, i + width) for i in range(0, rows, width)]
    eye = (
        lax.broadcasted_iota(jnp.int32, (DK, DK), 0) == lax.broadcasted_iota(jnp.int32, (DK, DK), 1)
    ).astype(F32)
    us, pus = [], []
    for at in spans:
        decays, carried, lower, strict = gates_of(pos[at], logd[at], width)
        key_dots = mm(k[at], k[at], 1, 1)
        inv = unit_inverse(beta[at] * decays * key_dots * strict)
        inv_ref[at, :] = inv
        u = mm(inv, beta[at] * v[at])
        y = mm(inv, (beta[at] * carried) * k[at])
        p = decays * mm(q[at], k[at], 1, 1)
        qt = carried * q[at] - mm(p, y)
        pus.append(mm(p, u))
        us.append(u)
        y_ref[at, :] = y
        qt_ref[at, :] = qt
        kf = final_of(decays, width) * k[at]
        for j in range(width // GROUP):
            g = slice(j * GROUP, (j + 1) * GROUP)
            index = at.start // GROUP + j
            end = carried[(j + 1) * GROUP - 1 : (j + 1) * GROUP, :]
            m_ref[index] = end * eye - mm(kf[g], y[g], 0, 0)
            n_ref[index] = mm(kf[g], u[g], 0, 0)
    state = jnp.zeros((DK, DV), F32)
    for index in range(rows // GROUP):
        state_ref[index] = state
        if index + 1 < rows // GROUP:
            state = mm(m_ref[index], state) + n_ref[index]
    for index in range(rows // GROUP):
        g = slice(index * GROUP, (index + 1) * GROUP)
        inner = slice((index * GROUP) % width, (index * GROUP) % width + GROUP)
        state = state_ref[index]
        wr_ref[g, :] = us[index * GROUP // width][inner] - mm(y_ref[g, :], state)
        o_ref[g, :] = mm(qt_ref[g, :], state) + pus[index * GROUP // width][inner]
    out = o_ref[...]
    ro = lax.rsqrt(jnp.mean(out * out, -1, keepdims=True) + NORM_EPS)
    gate = px_ref[:, HEADC:HEADG]
    mixed_ref[...] = (out * ro * hg_ref[...] * (gate * jax.nn.sigmoid(gate))).astype(BF)


def core_bwd_kernel(
    px_ref, taps_ref, par_ref, pos_ref, hg_ref, dm_ref,
    state_ref, inv_ref, wr_ref, y_ref, qt_ref, m_ref, o_ref,
    dpx_ref, dtaps_ref, dhg_ref, dpar_ref,
    dst_ref, do_ref, dq_ref, dk_ref, dv_ref, db_ref, dg_ref,
):
    rows = px_ref.shape[0]
    width = min(4 * GROUP, rows)
    groups = rows // GROUP
    out = o_ref[...]
    ro = lax.rsqrt(jnp.mean(out * out, -1, keepdims=True) + NORM_EPS)
    on = out * ro
    gate = px_ref[:, HEADC:HEADG]
    sg = jax.nn.sigmoid(gate)
    dm = dm_ref[...]
    dpx_ref[:, HEADC:HEADG] = (dm * on * hg_ref[...] * (sg * (1.0 + gate * (1.0 - sg)))).astype(BF)
    dgained = dm * (gate * sg)
    dhg_ref[...] = jnp.sum(dgained * on, 0, keepdims=True)
    don = dgained * hg_ref[...]
    do_ref[...] = ro * (don - on * jnp.mean(don * on, -1, keepdims=True))

    pos, x, conv, sig, qr, kr, rq, rk, q, k, v, beta, scale, shifted, logd = pre_stage(
        px_ref, taps_ref, par_ref, pos_ref
    )
    back = jnp.zeros((DK, DV), F32)
    for index in reversed(range(groups)):
        g = slice(index * GROUP, (index + 1) * GROUP)
        dst_ref[index] = back
        if index:
            back = mm(m_ref[index], back, 0, 0) + mm(qt_ref[g, :], do_ref[g, :], 0, 0)
    for start in range(0, rows, width):
        at = slice(start, start + width)
        decays, carried, lower, strict = gates_of(pos[at], logd[at], width)
        qs, ks, vs, bs = q[at], k[at], v[at], beta[at]
        key_dots = mm(ks, ks, 1, 1)
        query_dots = mm(qs, ks, 1, 1)
        final = final_of(decays, width)
        kf = final * ks
        do = do_ref[at, :]
        w = wr_ref[at, :]
        inv = inv_ref[at, :]
        parts_w, parts_os, parts_kf, lasts = [], [], [], []
        for j in range(width // GROUP):
            g = slice(j * GROUP, (j + 1) * GROUP)
            index = start // GROUP + j
            parts_w.append(mm(kf[g], dst_ref[index]))
            parts_os.append(mm(do[g], state_ref[index], 1, 1))
            parts_kf.append(mm(w[g], dst_ref[index], 1, 1))
            lasts.append(
                jnp.sum(jnp.sum(dst_ref[index] * state_ref[index], -1, keepdims=True), 0, keepdims=True)
            )
        dw = mm(decays * query_dots, do, 0, 0) + jnp.concatenate(parts_w, 0)
        dtar = mm(inv, dw, 0, 0)
        dts = jnp.concatenate(
            [
                mm(dtar[j * GROUP : (j + 1) * GROUP], state_ref[start // GROUP + j], 1, 1)
                for j in range(width // GROUP)
            ],
            0,
        )
        dos = jnp.concatenate(parts_os, 0)
        dkf = jnp.concatenate(parts_kf, 0)
        dp = mm(do, w, 1, 1)
        dlow = -mm(dtar, w, 1, 1) * strict
        dqk = decays * dp
        low_dots = decays * key_dots * dlow
        dkk = bs * decays * dlow
        dq_ref[at, :] = mm(dqk, ks) + carried * dos
        k_dts = jnp.sum(ks * dts, -1, keepdims=True)
        dk_ref[at, :] = (
            mm(dqk, qs, 0, 0)
            + mm(dkk, ks)
            + mm(dkk, ks, 0, 0)
            - (bs * carried) * dts
            + final * dkf
        )
        dv_ref[at, :] = bs * dtar
        db_ref[at, :] = (
            jnp.sum(dtar * vs, -1, keepdims=True)
            - carried * k_dts
            + jnp.sum(low_dots, -1, keepdims=True)
        )
        dfinal = jnp.sum(dkf * ks, -1, keepdims=True)
        dcar = jnp.sum(qs * dos, -1, keepdims=True) - bs * k_dts
        pair = query_dots * dqk + bs * low_dots
        ones = jnp.ones((width, DK), F32)
        row_at = lax.broadcasted_iota(jnp.int32, (width, 1), 0)
        fin = dfinal * final[:, :1]
        dcum = (
            jnp.broadcast_to(jnp.sum(pair, -1, keepdims=True) + dcar * carried - fin, (width, DK))
            - mm(pair, ones, 0, 0)
        )
        for j in range(width // GROUP):
            g = slice(j * GROUP, (j + 1) * GROUP)
            e = (j + 1) * GROUP - 1
            gain = lasts[j] * carried[e : e + 1, :] + jnp.sum(fin[g], 0, keepdims=True)
            dcum = dcum + jnp.where(row_at == e, gain, 0.0)
        dg_ref[at, :] = mm(lower, dcum, 0, 0)[:, :1]

    dqn = dq_ref[...] * DK ** (-0.5)
    dkn = dk_ref[...]
    dqr = rq * (dqn - qr * (rq * rq) * jnp.sum(dqn * qr, -1, keepdims=True))
    dkr = rk * (dkn - kr * (rk * rk) * jnp.sum(dkn * kr, -1, keepdims=True))
    dact = jnp.concatenate([dqr, dkr, dv_ref[...]], -1)
    dconv = dact * (sig * (1.0 + conv * (1.0 - sig)))
    dx = dconv * taps_ref[CONV - 1 : CONV, :]
    dtaps_ref[CONV - 1 : CONV, :] = jnp.sum(dconv * x, 0, keepdims=True)
    for s in range(1, CONV):
        used = dconv * (pos >= s).astype(F32)
        dx = dx + taps_ref[CONV - 1 - s : CONV - s, :] * shift_rows(used, -s)
        dtaps_ref[CONV - 1 - s : CONV - s, :] = jnp.sum(used * shift_rows(x, s), 0, keepdims=True)
    dpx_ref[:, :HEADC] = dx.astype(BF)
    db = db_ref[...] * beta * (1.0 - beta)
    dg = dg_ref[...]
    da = dg * scale * jax.nn.sigmoid(shifted)
    lane = lax.broadcasted_iota(jnp.int32, (rows, EXTRA), 1)
    dpx_ref[:, HEADG:] = jnp.where(lane == 0, db, jnp.where(lane == 1, da, 0.0)).astype(BF)
    one = lax.broadcasted_iota(jnp.int32, (1, EXTRA), 1)
    dpar_ref[...] = jnp.where(
        one == 0,
        jnp.sum(dg * logd, 0, keepdims=True),
        jnp.where(one == 1, jnp.sum(da, 0, keepdims=True), 0.0),
    )


def vspec():
    return pl.BlockSpec(memory_space=pltpu.VMEM)


def core_fwd(px, taps, par, pos, gain):
    rows = px.shape[0]
    groups = rows // GROUP
    width = min(4 * GROUP, rows)
    shape = jax.ShapeDtypeStruct
    return pl.pallas_call(
        core_fwd_kernel,
        name="core_fwd",
        out_shape=(
            shape((rows, DV), BF),
            shape((groups, DK, DV), F32),
            shape((rows, width), F32),
            shape((rows, DV), F32),
            shape((rows, DK), F32),
            shape((rows, DK), F32),
            shape((groups, DK, DK), F32),
            shape((rows, DV), F32),
        ),
        in_specs=[vspec(), vspec(), pl.BlockSpec(memory_space=pltpu.SMEM), vspec(), vspec()],
        out_specs=tuple(vspec() for _ in range(8)),
        scratch_shapes=[pltpu.VMEM((groups, DK, DV), F32)],
        compiler_params=pltpu.CompilerParams(vmem_limit_bytes=48 << 20),
    )(px, taps, par, pos, gain)


def core_bwd(px, taps, par, pos, gain, dm, saved):
    rows = px.shape[0]
    groups = rows // GROUP
    shape = jax.ShapeDtypeStruct
    return pl.pallas_call(
        core_bwd_kernel,
        name="core_bwd",
        out_shape=(
            shape((rows, HEADG + EXTRA), BF),
            shape((CONV, HEADC), F32),
            shape((1, DV), F32),
            shape((1, EXTRA), F32),
        ),
        in_specs=[vspec(), vspec(), pl.BlockSpec(memory_space=pltpu.SMEM)]
        + [vspec() for _ in range(3 + len(saved))],
        out_specs=tuple(vspec() for _ in range(4)),
        scratch_shapes=[
            pltpu.VMEM((groups, DK, DV), F32),
            pltpu.VMEM((rows, DV), F32),
            pltpu.VMEM((rows, DK), F32),
            pltpu.VMEM((rows, DK), F32),
            pltpu.VMEM((rows, DV), F32),
            pltpu.VMEM((rows, 1), F32),
            pltpu.VMEM((rows, 1), F32),
        ],
        compiler_params=pltpu.CompilerParams(vmem_limit_bytes=48 << 20),
    )(px, taps, par, pos, gain, dm, *saved)


def swap(value, axis, mask):
    count = lax.axis_size(axis)
    return lax.ppermute(value, axis, [(i, i ^ mask) for i in range(count)])


def put(buffer, piece, index, axis):
    return lax.dynamic_update_slice_in_dim(buffer, jnp.expand_dims(piece, axis), index, axis)


def take(buffer, index, axis):
    return lax.dynamic_index_in_dim(buffer, index, axis, keepdims=False)


def bits_of(axis):
    count = lax.axis_size(axis)
    assert count & (count - 1) == 0
    masks = []
    mask = count // 2
    while mask:
        masks.append(mask)
        mask //= 2
    return masks


def near_pieces(value, axis):
    pieces = {0: value}
    for mask in bits_of(axis):
        for m in list(pieces):
            pieces[m ^ mask] = swap(pieces[m], axis, mask)
    return [pieces[m] for m in range(lax.axis_size(axis))]


def ordered(pieces, axis):
    me = lax.axis_index(axis)
    out = jnp.zeros((len(pieces),) + pieces[0].shape, pieces[0].dtype)
    for m, piece in enumerate(pieces):
        out = put(out, piece, me ^ m, 0)
    return out


def gather_rows(value, axis):
    out = ordered(near_pieces(value, axis), axis)
    return out.reshape((-1,) + value.shape[1:])


def reduce_rows(value, axis):
    me = lax.axis_index(axis)
    count = value.shape[0]
    part = value
    for mask in bits_of(axis):
        halves = part.reshape((2, -1) + value.shape[1:])
        bit = (me // mask) % 2
        away = swap(take(halves, 1 - bit, 0).astype(BF), axis, mask)
        part = take(halves, bit, 0).astype(F32) + away.astype(F32)
    return part[0]


def trade(value, axis):
    me = lax.axis_index(axis)
    pieces = [take(value, me, 0)]
    for m in range(1, value.shape[0]):
        pieces.append(swap(take(value, me ^ m, 0), axis, m))
    return ordered(pieces, axis)


def gather_far(value, axis):
    count = lax.axis_size(axis)
    k, r, w = value.shape
    if count > 8 or count < 4 or r % 32:
        return lax.all_gather(value, axis, axis=1, tiled=True)
    me = lax.axis_index(axis)
    far, near = me // 2, me % 2
    half = r // 2
    first, second = value[:, :half], value[:, half:]
    out = jnp.zeros((k, count // 2, 2, 2, half, w), value.dtype)

    def place(out, piece, f, n, h):
        piece = piece.reshape((k, piece.size // (k * half * w), 1, 1, half, w)) if piece.ndim == 4 else piece[:, None, None, None]
        return lax.dynamic_update_slice(out, piece, (0, f, n, h, 0, 0))

    column = jnp.zeros((k, count // 2, half, w), value.dtype)
    column = put(column, first, far, 1)
    other = swap(second, axis, 1)
    pair = put(put(jnp.zeros((k, 2, half, w), value.dtype), second, near, 1), other, 1 - near, 1)
    for m in range(1, count // 2):
        column = put(column, swap(first, axis, 2 * m), far ^ m, 1)
    beside = swap(column, axis, 1)
    zero = jnp.zeros_like(far)
    out = lax.dynamic_update_slice(out, column[:, :, None, None], (zero, zero, near, zero, zero, zero))
    out = lax.dynamic_update_slice(out, beside[:, :, None, None], (zero, zero, 1 - near, zero, zero, zero))
    one = zero + 1
    out = lax.dynamic_update_slice(out, pair[:, None, :, None], (zero, far, zero, one, zero, zero))
    for m in range(1, count // 2):
        got = swap(pair, axis, 2 * m)
        out = lax.dynamic_update_slice(out, got[:, None, :, None], (zero, far ^ m, zero, one, zero, zero))
    return out.reshape(k, count * r, w)


def reduce_far(value, axis):
    count = lax.axis_size(axis)
    k, rows, w = value.shape
    r = rows // count
    if count > 8 or count < 4 or r % 32:
        return lax.psum_scatter(value, axis, scatter_dimension=1, tiled=True).astype(F32)
    me = lax.axis_index(axis)
    far, near = me // 2, me % 2
    half = r // 2
    blocks = value.reshape(k, count // 2, 2, 2, half, w)
    first, second = blocks[:, :, :, 0], blocks[:, :, :, 1]
    got = swap(take(first, 1 - near, 2), axis, 1)
    column = take(first, near, 2).astype(F32) + got.astype(F32)
    pair = take(second, far, 1).astype(F32)
    for m in range(1, count // 2):
        pair = pair + swap(take(second, far ^ m, 1), axis, 2 * m).astype(F32)
    sent = column.astype(BF)
    total_a = take(column, far, 1)
    for m in range(1, count // 2):
        total_a = total_a + swap(take(sent, far ^ m, 1), axis, 2 * m).astype(F32)
    back = swap(take(pair, 1 - near, 1).astype(BF), axis, 1)
    total_b = take(pair, near, 1) + back.astype(F32)
    return jnp.concatenate([total_a, total_b], axis=1)


def sum_everywhere(value, axes):
    for axis in axes:
        count = lax.axis_size(axis)
        if count & (count - 1):
            value = lax.psum(value, axis)
            continue
        for mask in bits_of(axis):
            value = value + swap(value, axis, mask)
    return value


def doc_positions(lengths, count):
    ends = jnp.cumsum(lengths, axis=-1)
    starts = ends - lengths
    places = jnp.arange(count, dtype=jnp.int32)
    owner = jnp.max(jnp.where(starts[None, :] <= places[:, None], starts[None, :], 0), axis=-1)
    return places - owner


def adamw(weights, moment, square, grads):
    new_moment = beta_one * moment + (1.0 - beta_one) * grads
    new_square = beta_two * square + (1.0 - beta_two) * grads * grads
    corrected = new_moment / (1.0 - beta_one**STEP)
    scaled = new_square / (1.0 - beta_two**STEP)
    new_weights = weights - learn_rate * (
        corrected / (jnp.sqrt(scaled) + adam_eps) + weight_decay * weights
    )
    return (new_weights, new_moment, new_square)


def dot(a, b, lhs=1, rhs=0):
    return lax.dot_general(a, b, (((lhs,), (rhs,)), ((), ())), preferred_element_type=F32)


def local(
    activations, cotangent, live_slots, doc_lengths,
    inproj, mom_inproj, sqr_inproj,
    gateproj, mom_gateproj, sqr_gateproj,
    outproj, mom_outproj, sqr_outproj,
    mlp_gate, mom_mlp_gate, sqr_mlp_gate,
    mlp_up, mom_mlp_up, sqr_mlp_up,
    mlp_down, mom_mlp_down, sqr_mlp_down,
    vectors, mom_vectors, sqr_vectors,
    headvec, mom_headvec, sqr_headvec,
):
    n_ctx = lax.axis_size("ctx")
    me = lax.axis_index("ctx")
    assert n_ctx == H and activations.shape[0] == 1
    length = activations.shape[1]
    rows = inproj.shape[0]
    ff = mlp_gate.shape[1] // n_ctx
    per_row = vectors.shape[0] // rows
    vec_at = 2
    assert per_row * rows == vectors.shape[0] and vec_at + per_row <= EXTRA
    live = live_slots[0].astype(F32)
    act_own, cot_own = activations[0], cotangent[0]

    in_b = inproj.astype(BF)
    gp_b = gateproj.astype(BF)
    vec_b = vectors.astype(BF).reshape(rows, per_row)
    pad_b = jnp.zeros((rows, EXTRA - vec_at - per_row), BF)
    kq, vq, gq = H * DK, 2 * H * DK, 2 * H * DK + H * DV

    def in_slice(c):
        return jnp.concatenate(
            [
                in_b[:, c * DK : (c + 1) * DK],
                in_b[:, kq + c * DK : kq + (c + 1) * DK],
                in_b[:, vq + c * DV : vq + (c + 1) * DV],
                in_b[:, gq + c * DV : gq + (c + 1) * DV],
                gp_b[:, c : c + 1],
                gp_b[:, H + c : H + c + 1],
                vec_b,
                pad_b,
            ],
            axis=1,
        )

    w_in = trade(jnp.stack([in_slice(c) for c in range(n_ctx)]), "ctx").reshape(1, n_ctx * rows, -1)
    full_in = gather_far(w_in, "dp")[0]
    x_full = gather_rows(act_own, "ctx")
    out_t = outproj.T.astype(BF)
    w_out = trade(jnp.stack([out_t[:, c * DV : (c + 1) * DV] for c in range(n_ctx)]), "ctx")
    full_out = gather_far(w_out.reshape(1, n_ctx * rows, DV), "dp")[0]
    down_t = mlp_down.T
    w_mlp = jnp.stack(
        [
            jnp.stack([w[:, c * ff : (c + 1) * ff].astype(BF) for w in (mlp_gate, mlp_up, down_t)])
            for c in range(n_ctx)
        ]
    )
    w_mlp = jnp.swapaxes(trade(w_mlp, "ctx"), 0, 1).reshape(3, n_ctx * rows, ff)
    full_mlp = gather_far(w_mlp, "dp")
    full_wg, full_wu, full_wd = full_mlp[0], full_mlp[1], full_mlp[2]
    outs_near = near_pieces(full_out, "ctx")
    cot_full = gather_rows(cot_own, "ctx")

    vec_float = full_in[:, HEADG + vec_at : HEADG + vec_at + per_row].astype(F32).reshape(-1)
    norm_gain = vec_float[:D]
    taps_all = vec_float[D : D + CONV * CONVC].reshape(CONV, CONVC)
    mlp_gain = vec_float[D + CONV * CONVC :]
    head_gain = headvec[:DV]

    def my_taps(first, size):
        return lax.dynamic_slice_in_dim(taps_all, first + me * size, size, 1)

    taps = jnp.concatenate([my_taps(0, DK), my_taps(kq, DK), my_taps(vq, DV)], axis=1)
    par = jnp.stack(
        [
            lax.dynamic_index_in_dim(headvec, DV + me, 0, keepdims=False),
            lax.dynamic_index_in_dim(headvec, DV + H + me, 0, keepdims=False),
        ]
    )
    total = n_ctx * length
    pos = doc_positions(doc_lengths[0], total)[:, None]

    xf = x_full.astype(F32)
    inv_rms = lax.rsqrt(jnp.mean(xf * xf, -1, keepdims=True) + NORM_EPS)
    unit = xf * inv_rms
    normed = (unit * norm_gain).astype(BF)
    px = dot(normed, full_in)
    mixed, *saved = core_fwd(px, taps, par, pos, head_gain[None, :])
    branch = 0.0
    for piece, weight in zip(near_pieces(mixed, "ctx"), outs_near):
        branch = branch + dot(piece, weight, 1, 1)
    resid = xf + live * branch
    inv_two = lax.rsqrt(jnp.mean(resid * resid, -1, keepdims=True) + NORM_EPS)
    unit_two = resid * inv_two
    normed_two = (unit_two * mlp_gain).astype(BF)

    hgate = dot(normed_two, full_wg)
    hup = dot(normed_two, full_wu)
    sigma = jax.nn.sigmoid(hgate)
    silu_gate = hgate * sigma
    hidden = (silu_gate * hup).astype(BF)
    g_mlp = (cot_full.astype(F32) * live).astype(BF)
    d_hidden = dot(g_mlp, full_wd)
    d_hgate = (d_hidden * hup * sigma * (1.0 + hgate * (1.0 - sigma))).astype(BF)
    d_hup = (d_hidden * silu_gate).astype(BF)
    d_two = dot(d_hgate, full_wg, 1, 1) + dot(d_hup, full_wu, 1, 1)
    d_gain_two = jnp.sum(d_two * unit_two, axis=0)
    d_two_own = reduce_rows(d_two.astype(BF).reshape(n_ctx, length, D), "ctx")

    def own_rows(value):
        return lax.dynamic_slice_in_dim(value, me * length, length, 0)

    x_own = act_own.astype(F32)
    resid_own = own_rows(resid)
    inv_own = lax.rsqrt(jnp.mean(resid_own * resid_own, -1, keepdims=True) + NORM_EPS)
    unit_own = resid_own * inv_own
    d_unit_two = d_two_own * mlp_gain
    d_resid = cot_own.astype(F32) + inv_own * (
        d_unit_two - unit_own * jnp.mean(d_unit_two * unit_own, -1, keepdims=True)
    )
    g_own = (d_resid * live).astype(BF)
    g_branch = gather_rows(g_own, "ctx")

    mlp_part = dot(hidden, full_wd, 1, 1).astype(BF)
    mlp_own = reduce_rows(mlp_part.reshape(n_ctx, length, D), "ctx")
    block_out = (resid_own + live * mlp_own).astype(BF)

    grad_mlp = jnp.stack(
        [
            dot(normed_two, d_hgate, 0, 0).astype(BF),
            dot(normed_two, d_hup, 0, 0).astype(BF),
            dot(g_mlp, hidden, 0, 0).astype(BF),
        ]
    )

    d_mixed = dot(g_branch, full_out)
    grad_out = dot(g_branch, mixed, 0, 0).astype(BF)
    d_px, d_taps, d_hgain, d_par = core_bwd(px, taps, par, pos, head_gain[None, :], d_mixed, saved)
    d_normed = dot(d_px, full_in, 1, 1)
    d_gain = jnp.sum(d_normed * unit, axis=0)
    d_taps_all = jnp.zeros((CONV, CONVC), F32)
    for piece, first, size in (
        (d_taps[:, :DK], 0, DK),
        (d_taps[:, DK : 2 * DK], kq, DK),
        (d_taps[:, 2 * DK :], vq, DV),
    ):
        d_taps_all = lax.dynamic_update_slice(d_taps_all, piece, (0, first + me * size))
    grad_vec = jnp.concatenate([d_gain, d_taps_all.reshape(-1), d_gain_two]).reshape(-1, per_row)
    grad_in = dot(normed, d_px, 0, 0)
    grad_in = jnp.concatenate(
        [
            grad_in[:, : HEADG + vec_at],
            grad_vec,
            jnp.zeros((grad_in.shape[0], EXTRA - vec_at - per_row), F32),
        ],
        axis=1,
    ).astype(BF)

    def to_owner(value):
        part = reduce_far(value, "dp")
        k, _, w = part.shape
        part = jnp.swapaxes(part.reshape(k, n_ctx, rows, w), 0, 1).astype(BF)
        return trade(part, "ctx").astype(F32)

    own_mlp = to_owner(grad_mlp)
    own_out = to_owner(grad_out[None])[:, 0]
    own_in = to_owner(grad_in[None])[:, 0]

    def beside(value, first, size):
        return [value[c, :, first : first + size] for c in range(n_ctx)]

    owned_in = jnp.concatenate(
        beside(own_in, 0, DK) + beside(own_in, DK, DK) + beside(own_in, 2 * DK, DV) + beside(own_in, HEADC, DV),
        axis=1,
    )
    owned_ab = jnp.concatenate(beside(own_in, HEADG, 1) + beside(own_in, HEADG + 1, 1), axis=1)
    owned_vec = jnp.sum(own_in[:, :, HEADG + vec_at : HEADG + vec_at + per_row], axis=0).reshape(-1)
    owned_out = jnp.concatenate(beside(own_out, 0, DV), axis=1).T
    owned_wg, owned_wu, owned_wd_t = (
        jnp.concatenate([own_mlp[c, k] for c in range(n_ctx)], axis=1) for k in range(3)
    )
    owned_wd = owned_wd_t.T
    at_head = jnp.arange(H) == me
    grad_small = jnp.concatenate(
        [d_hgain[0], jnp.where(at_head, d_par[0, 0], 0.0), jnp.where(at_head, d_par[0, 1], 0.0)]
    )
    summed_small = sum_everywhere(grad_small, ("ctx", "dp"))

    d_normed_own = reduce_rows(d_normed.astype(BF).reshape(n_ctx, length, D), "ctx")
    inv_x = lax.rsqrt(jnp.mean(x_own * x_own, -1, keepdims=True) + NORM_EPS)
    unit_x = x_own * inv_x
    d_unit = d_normed_own * norm_gain
    input_grad = (
        d_resid + inv_x * (d_unit - unit_x * jnp.mean(d_unit * unit_x, -1, keepdims=True))
    ).astype(BF)

    n_in, nm_in, ns_in = adamw(inproj, mom_inproj, sqr_inproj, owned_in)
    n_ab, nm_ab, ns_ab = adamw(gateproj, mom_gateproj, sqr_gateproj, owned_ab)
    n_out, nm_out, ns_out = adamw(outproj, mom_outproj, sqr_outproj, owned_out)
    n_wg, nm_wg, ns_wg = adamw(mlp_gate, mom_mlp_gate, sqr_mlp_gate, owned_wg)
    n_wu, nm_wu, ns_wu = adamw(mlp_up, mom_mlp_up, sqr_mlp_up, owned_wu)
    n_wd, nm_wd, ns_wd = adamw(mlp_down, mom_mlp_down, sqr_mlp_down, owned_wd)
    n_vec, nm_vec, ns_vec = adamw(vectors, mom_vectors, sqr_vectors, owned_vec)
    n_small, nm_small, ns_small = adamw(headvec, mom_headvec, sqr_headvec, summed_small)
    return (
        block_out[None], input_grad[None],
        owned_in, owned_ab, owned_out, owned_wg, owned_wu, owned_wd, owned_vec, summed_small,
        n_in, nm_in, ns_in,
        n_ab, nm_ab, ns_ab,
        n_out, nm_out, ns_out,
        n_wg, nm_wg, ns_wg,
        n_wu, nm_wu, ns_wu,
        n_wd, nm_wd, ns_wd,
        n_vec, nm_vec, ns_vec,
        n_small, nm_small, ns_small,
    )


def solution(mesh):
    rows = P(("dp", "ctx"), None)
    cols = P(None, ("dp", "ctx"))
    flat = P(("dp", "ctx"))
    tokens = P("dp", "ctx", None)
    params = (rows,) * 6 + (cols,) * 3 + (rows,) * 6 + (cols,) * 3 + (flat,) * 3 + (P(),) * 3
    grads = (rows, rows, cols, rows, rows, cols, flat, P())
    return jax.shard_map(
        local,
        mesh=mesh,
        in_specs=(tokens, tokens, P("dp"), P("dp", None)) + params,
        out_specs=(tokens, tokens) + grads + params,
        check_vma=False,
    )
```

```python
import jax
import jax.numpy as jnp
from jax import lax
from jax.experimental import pallas as pl
from jax.experimental.pallas import tpu as pltpu
from jax.sharding import PartitionSpec as P

D = 1024
H = 4
DK = 128
DV = 256
CONV = 4
GROUP = 64
STEP = 5
CONVC = 2048

NORM_EPS = 1e-06
beta_one = 0.9
beta_two = 0.999
learn_rate = 0.01
weight_decay = 0.1
adam_eps = 1e-08

F32 = jnp.float32
BF = jnp.bfloat16
EXACT = lax.Precision.HIGHEST

HEADQ = DK
HEADC = 2 * DK + DV
HEADG = HEADC + DV
EXTRA = 128


def mm(a, b, lhs=1, rhs=0):
    return lax.dot_general(
        a, b, (((lhs,), (rhs,)), ((), ())), precision=EXACT, preferred_element_type=F32
    )


def shift_rows(value, steps):
    return pltpu.roll(value, steps % value.shape[0], axis=0)


def pre_stage(px_ref, taps_ref, par_ref, pos_ref):
    rows = px_ref.shape[0]
    pos = pos_ref[...]
    x = px_ref[:, :HEADC]
    conv = x * taps_ref[CONV - 1 : CONV, :]
    for s in range(1, CONV):
        valid = (pos >= s).astype(F32)
        conv = conv + taps_ref[CONV - 1 - s : CONV - s, :] * (shift_rows(x, s) * valid)
    sig = jax.nn.sigmoid(conv)
    act = conv * sig
    qr = act[:, :DK]
    kr = act[:, DK : 2 * DK]
    v = act[:, 2 * DK :]
    rq = lax.rsqrt(jnp.sum(qr * qr, -1, keepdims=True) + NORM_EPS)
    rk = lax.rsqrt(jnp.sum(kr * kr, -1, keepdims=True) + NORM_EPS)
    q = qr * rq * DK ** (-0.5)
    k = kr * rk
    mix = px_ref[:, HEADG : HEADG + EXTRA]
    lane = lax.broadcasted_iota(jnp.int32, (rows, EXTRA), 1)
    b_raw = jnp.sum(jnp.where(lane == 0, mix, 0.0), -1, keepdims=True)
    a_raw = jnp.sum(jnp.where(lane == 1, mix, 0.0), -1, keepdims=True)
    beta = jax.nn.sigmoid(b_raw)
    scale = -jnp.exp(jnp.zeros((rows, 1), F32) + par_ref[0])
    shifted = a_raw + par_ref[1]
    soft = jnp.maximum(shifted, 0.0) + jnp.log1p(jnp.exp(-jnp.abs(shifted)))
    logd = scale * soft
    return pos, x, conv, sig, qr, kr, rq, rk, q, k, v, beta, scale, shifted, logd


def block_masks(width):
    row = lax.broadcasted_iota(jnp.int32, (width, width), 0)
    col = lax.broadcasted_iota(jnp.int32, (width, width), 1)
    same = (row // GROUP) == (col // GROUP)
    return row, col, same


def gates_of(pos, logd, width):
    row, col, same = block_masks(width)
    lower = ((row >= col) & same).astype(F32)
    lb = jnp.broadcast_to(logd, (width, width))
    cum_t = mm(lower, lb)
    cum_i = mm(lb, lower, 0, 1)
    keep = ((row >= col) & same & (pos >= row - col)).astype(F32)
    decays = jnp.exp(jnp.minimum(cum_t - cum_i, 0.0)) * keep
    at = lax.broadcasted_iota(jnp.int32, (width, 1), 0) % GROUP
    carried = jnp.exp(cum_t[:, :1]) * (pos >= at + 1).astype(F32)
    strict = (row > col).astype(F32)
    return decays, carried, lower, strict


def unit_inverse(low):
    width = low.shape[0]
    row, col, same = block_masks(width)
    size = 1
    out = None
    while size < GROUP:
        join = (
            ((row // (2 * size)) == (col // (2 * size)))
            & ((row // size) % 2 == 1)
            & ((col // size) % 2 == 0)
        )
        part = jnp.where(join, low, 0.0)
        if out is None:
            out = (row == col).astype(F32) - part
        else:
            out = out - mm(mm(out, part), out)
        size *= 2
    return out


def final_of(decays, width):
    row, col, same = block_masks(width)
    last = ((col % GROUP) == GROUP - 1) & same
    pick = jnp.where((row % GROUP) == GROUP - 1, decays, 0.0)
    ones = jnp.ones((width, DK), F32)
    return mm(pick, ones, 0, 0)


def core_fwd_kernel(
    px_ref, taps_ref, par_ref, pos_ref, hg_ref,
    mixed_ref, state_ref, inv_ref, wr_ref, y_ref, qt_ref, m_ref, o_ref,
    n_ref,
):
    rows = px_ref.shape[0]
    width = min(4 * GROUP, rows)
    pos, x, conv, sig, qr, kr, rq, rk, q, k, v, beta, scale, shifted, logd = pre_stage(
        px_ref, taps_ref, par_ref, pos_ref
    )
    spans = [slice(i, i + width) for i in range(0, rows, width)]
    eye = (
        lax.broadcasted_iota(jnp.int32, (DK, DK), 0) == lax.broadcasted_iota(jnp.int32, (DK, DK), 1)
    ).astype(F32)
    us, pus = [], []
    for at in spans:
        decays, carried, lower, strict = gates_of(pos[at], logd[at], width)
        key_dots = mm(k[at], k[at], 1, 1)
        inv = unit_inverse(beta[at] * decays * key_dots * strict)
        inv_ref[at, :] = inv
        u = mm(inv, beta[at] * v[at])
        y = mm(inv, (beta[at] * carried) * k[at])
        p = decays * mm(q[at], k[at], 1, 1)
        qt = carried * q[at] - mm(p, y)
        pus.append(mm(p, u))
        us.append(u)
        y_ref[at, :] = y
        qt_ref[at, :] = qt
        kf = final_of(decays, width) * k[at]
        for j in range(width // GROUP):
            g = slice(j * GROUP, (j + 1) * GROUP)
            index = at.start // GROUP + j
            end = carried[(j + 1) * GROUP - 1 : (j + 1) * GROUP, :]
            m_ref[index] = end * eye - mm(kf[g], y[g], 0, 0)
            n_ref[index] = mm(kf[g], u[g], 0, 0)
    state = jnp.zeros((DK, DV), F32)
    for index in range(rows // GROUP):
        state_ref[index] = state
        if index + 1 < rows // GROUP:
            state = mm(m_ref[index], state) + n_ref[index]
    for index in range(rows // GROUP):
        g = slice(index * GROUP, (index + 1) * GROUP)
        inner = slice((index * GROUP) % width, (index * GROUP) % width + GROUP)
        state = state_ref[index]
        wr_ref[g, :] = us[index * GROUP // width][inner] - mm(y_ref[g, :], state)
        o_ref[g, :] = mm(qt_ref[g, :], state) + pus[index * GROUP // width][inner]
    out = o_ref[...]
    ro = lax.rsqrt(jnp.mean(out * out, -1, keepdims=True) + NORM_EPS)
    gate = px_ref[:, HEADC:HEADG]
    mixed_ref[...] = (out * ro * hg_ref[...] * (gate * jax.nn.sigmoid(gate))).astype(BF)


def core_bwd_kernel(
    px_ref, taps_ref, par_ref, pos_ref, hg_ref, dm_ref,
    state_ref, inv_ref, wr_ref, y_ref, qt_ref, m_ref, o_ref,
    dpx_ref, dtaps_ref, dhg_ref, dpar_ref,
    dst_ref, do_ref, dq_ref, dk_ref, dv_ref, db_ref, dg_ref,
):
    rows = px_ref.shape[0]
    width = min(4 * GROUP, rows)
    groups = rows // GROUP
    out = o_ref[...]
    ro = lax.rsqrt(jnp.mean(out * out, -1, keepdims=True) + NORM_EPS)
    on = out * ro
    gate = px_ref[:, HEADC:HEADG]
    sg = jax.nn.sigmoid(gate)
    dm = dm_ref[...]
    dpx_ref[:, HEADC:HEADG] = (dm * on * hg_ref[...] * (sg * (1.0 + gate * (1.0 - sg)))).astype(BF)
    dgained = dm * (gate * sg)
    dhg_ref[...] = jnp.sum(dgained * on, 0, keepdims=True)
    don = dgained * hg_ref[...]
    do_ref[...] = ro * (don - on * jnp.mean(don * on, -1, keepdims=True))

    pos, x, conv, sig, qr, kr, rq, rk, q, k, v, beta, scale, shifted, logd = pre_stage(
        px_ref, taps_ref, par_ref, pos_ref
    )
    back = jnp.zeros((DK, DV), F32)
    for index in reversed(range(groups)):
        g = slice(index * GROUP, (index + 1) * GROUP)
        dst_ref[index] = back
        if index:
            back = mm(m_ref[index], back, 0, 0) + mm(qt_ref[g, :], do_ref[g, :], 0, 0)
    for start in range(0, rows, width):
        at = slice(start, start + width)
        decays, carried, lower, strict = gates_of(pos[at], logd[at], width)
        qs, ks, vs, bs = q[at], k[at], v[at], beta[at]
        key_dots = mm(ks, ks, 1, 1)
        query_dots = mm(qs, ks, 1, 1)
        final = final_of(decays, width)
        kf = final * ks
        do = do_ref[at, :]
        w = wr_ref[at, :]
        inv = inv_ref[at, :]
        parts_w, parts_os, parts_kf, lasts = [], [], [], []
        for j in range(width // GROUP):
            g = slice(j * GROUP, (j + 1) * GROUP)
            index = start // GROUP + j
            parts_w.append(mm(kf[g], dst_ref[index]))
            parts_os.append(mm(do[g], state_ref[index], 1, 1))
            parts_kf.append(mm(w[g], dst_ref[index], 1, 1))
            lasts.append(
                jnp.sum(jnp.sum(dst_ref[index] * state_ref[index], -1, keepdims=True), 0, keepdims=True)
            )
        dw = mm(decays * query_dots, do, 0, 0) + jnp.concatenate(parts_w, 0)
        dtar = mm(inv, dw, 0, 0)
        dts = jnp.concatenate(
            [
                mm(dtar[j * GROUP : (j + 1) * GROUP], state_ref[start // GROUP + j], 1, 1)
                for j in range(width // GROUP)
            ],
            0,
        )
        dos = jnp.concatenate(parts_os, 0)
        dkf = jnp.concatenate(parts_kf, 0)
        dp = mm(do, w, 1, 1)
        dlow = -mm(dtar, w, 1, 1) * strict
        dqk = decays * dp
        low_dots = decays * key_dots * dlow
        dkk = bs * decays * dlow
        dq_ref[at, :] = mm(dqk, ks) + carried * dos
        k_dts = jnp.sum(ks * dts, -1, keepdims=True)
        dk_ref[at, :] = (
            mm(dqk, qs, 0, 0)
            + mm(dkk, ks)
            + mm(dkk, ks, 0, 0)
            - (bs * carried) * dts
            + final * dkf
        )
        dv_ref[at, :] = bs * dtar
        db_ref[at, :] = (
            jnp.sum(dtar * vs, -1, keepdims=True)
            - carried * k_dts
            + jnp.sum(low_dots, -1, keepdims=True)
        )
        dfinal = jnp.sum(dkf * ks, -1, keepdims=True)
        dcar = jnp.sum(qs * dos, -1, keepdims=True) - bs * k_dts
        pair = query_dots * dqk + bs * low_dots
        ones = jnp.ones((width, DK), F32)
        row_at = lax.broadcasted_iota(jnp.int32, (width, 1), 0)
        fin = dfinal * final[:, :1]
        dcum = (
            jnp.broadcast_to(jnp.sum(pair, -1, keepdims=True) + dcar * carried - fin, (width, DK))
            - mm(pair, ones, 0, 0)
        )
        for j in range(width // GROUP):
            g = slice(j * GROUP, (j + 1) * GROUP)
            e = (j + 1) * GROUP - 1
            gain = lasts[j] * carried[e : e + 1, :] + jnp.sum(fin[g], 0, keepdims=True)
            dcum = dcum + jnp.where(row_at == e, gain, 0.0)
        dg_ref[at, :] = mm(lower, dcum, 0, 0)[:, :1]

    dqn = dq_ref[...] * DK ** (-0.5)
    dkn = dk_ref[...]
    dqr = rq * (dqn - qr * (rq * rq) * jnp.sum(dqn * qr, -1, keepdims=True))
    dkr = rk * (dkn - kr * (rk * rk) * jnp.sum(dkn * kr, -1, keepdims=True))
    dact = jnp.concatenate([dqr, dkr, dv_ref[...]], -1)
    dconv = dact * (sig * (1.0 + conv * (1.0 - sig)))
    dx = dconv * taps_ref[CONV - 1 : CONV, :]
    dtaps_ref[CONV - 1 : CONV, :] = jnp.sum(dconv * x, 0, keepdims=True)
    for s in range(1, CONV):
        used = dconv * (pos >= s).astype(F32)
        dx = dx + taps_ref[CONV - 1 - s : CONV - s, :] * shift_rows(used, -s)
        dtaps_ref[CONV - 1 - s : CONV - s, :] = jnp.sum(used * shift_rows(x, s), 0, keepdims=True)
    dpx_ref[:, :HEADC] = dx.astype(BF)
    db = db_ref[...] * beta * (1.0 - beta)
    dg = dg_ref[...]
    da = dg * scale * jax.nn.sigmoid(shifted)
    lane = lax.broadcasted_iota(jnp.int32, (rows, EXTRA), 1)
    dpx_ref[:, HEADG:] = jnp.where(lane == 0, db, jnp.where(lane == 1, da, 0.0)).astype(BF)
    one = lax.broadcasted_iota(jnp.int32, (1, EXTRA), 1)
    dpar_ref[...] = jnp.where(
        one == 0,
        jnp.sum(dg * logd, 0, keepdims=True),
        jnp.where(one == 1, jnp.sum(da, 0, keepdims=True), 0.0),
    )


def vspec():
    return pl.BlockSpec(memory_space=pltpu.VMEM)


def core_fwd(px, taps, par, pos, gain):
    rows = px.shape[0]
    groups = rows // GROUP
    width = min(4 * GROUP, rows)
    shape = jax.ShapeDtypeStruct
    return pl.pallas_call(
        core_fwd_kernel,
        name="core_fwd",
        out_shape=(
            shape((rows, DV), BF),
            shape((groups, DK, DV), F32),
            shape((rows, width), F32),
            shape((rows, DV), F32),
            shape((rows, DK), F32),
            shape((rows, DK), F32),
            shape((groups, DK, DK), F32),
            shape((rows, DV), F32),
        ),
        in_specs=[vspec(), vspec(), pl.BlockSpec(memory_space=pltpu.SMEM), vspec(), vspec()],
        out_specs=tuple(vspec() for _ in range(8)),
        scratch_shapes=[pltpu.VMEM((groups, DK, DV), F32)],
        compiler_params=pltpu.CompilerParams(vmem_limit_bytes=48 << 20),
    )(px, taps, par, pos, gain)


def core_bwd(px, taps, par, pos, gain, dm, saved):
    rows = px.shape[0]
    groups = rows // GROUP
    shape = jax.ShapeDtypeStruct
    return pl.pallas_call(
        core_bwd_kernel,
        name="core_bwd",
        out_shape=(
            shape((rows, HEADG + EXTRA), BF),
            shape((CONV, HEADC), F32),
            shape((1, DV), F32),
            shape((1, EXTRA), F32),
        ),
        in_specs=[vspec(), vspec(), pl.BlockSpec(memory_space=pltpu.SMEM)]
        + [vspec() for _ in range(3 + len(saved))],
        out_specs=tuple(vspec() for _ in range(4)),
        scratch_shapes=[
            pltpu.VMEM((groups, DK, DV), F32),
            pltpu.VMEM((rows, DV), F32),
            pltpu.VMEM((rows, DK), F32),
            pltpu.VMEM((rows, DK), F32),
            pltpu.VMEM((rows, DV), F32),
            pltpu.VMEM((rows, 1), F32),
            pltpu.VMEM((rows, 1), F32),
        ],
        compiler_params=pltpu.CompilerParams(vmem_limit_bytes=48 << 20),
    )(px, taps, par, pos, gain, dm, *saved)


TILE = 256


def mlp_grad_kernel(two_ref, cot_ref, dg_ref, du_ref, hid_ref, out_ref, turned_ref):
    step = pl.program_id(0)
    third = pl.num_programs(0) // 3

    @pl.when(step == 0)
    def _():
        turned_ref[...] = two_ref[...].T

    @pl.when(step == 2 * third)
    def _():
        turned_ref[...] = cot_ref[...].T

    right = jnp.where(step < third, dg_ref[...], jnp.where(step < 2 * third, du_ref[...], hid_ref[...]))
    out_ref[...] = lax.dot_general(
        turned_ref[...], right, (((1,), (0,)), ((), ())), preferred_element_type=F32
    ).astype(BF)


def mlp_grad(two, cot, dg, du, hid):
    rows, width = dg.shape
    depth = two.shape[1]
    third = width // TILE
    whole = pl.BlockSpec((rows, depth), lambda i: (0, 0))

    def tile(first):
        return pl.BlockSpec((rows, TILE), lambda i: (0, jnp.clip(i - first, 0, third - 1)))

    return pl.pallas_call(
        mlp_grad_kernel,
        name="mlp_grad",
        grid=(3 * third,),
        out_shape=jax.ShapeDtypeStruct((depth, 3 * width), BF),
        in_specs=[whole, whole, tile(0), tile(third), tile(2 * third)],
        out_specs=pl.BlockSpec((depth, TILE), lambda i: (0, i)),
        scratch_shapes=[pltpu.VMEM((depth, rows), BF)],
        compiler_params=pltpu.CompilerParams(vmem_limit_bytes=32 << 20),
    )(two, cot, dg, du, hid)


def mix_grad_kernel(norm_ref, dpx_ref, branch_ref, mixed_ref, vec_ref, out_ref, turned_ref):
    step = pl.program_id(0)
    first = (HEADG + EXTRA) // EXTRA

    @pl.when(step == 0)
    def _():
        turned_ref[...] = norm_ref[...].T

    @pl.when(step == first)
    def _():
        turned_ref[...] = branch_ref[...].T

    right = jnp.where(step < first, dpx_ref[...], mixed_ref[...])
    got = lax.dot_general(
        turned_ref[...], right, (((1,), (0,)), ((), ())), preferred_element_type=F32
    )
    out_ref[...] = got.astype(BF)

    @pl.when(step == first - 1)
    def _():
        lane = lax.broadcasted_iota(jnp.int32, got.shape, 1)
        out_ref[...] = jnp.where(lane < EXTRA // 2, got, vec_ref[...]).astype(BF)


def mix_grad(normed, dpx, branch, mixed, vec):
    rows, depth = normed.shape
    first = dpx.shape[1] // EXTRA
    steps = first + mixed.shape[1] // EXTRA
    whole = pl.BlockSpec((rows, depth), lambda i: (0, 0))
    return pl.pallas_call(
        mix_grad_kernel,
        name="mix_grad",
        grid=(steps,),
        out_shape=jax.ShapeDtypeStruct((depth, steps * EXTRA), BF),
        in_specs=[
            whole,
            pl.BlockSpec((rows, EXTRA), lambda i: (0, jnp.minimum(i, first - 1))),
            whole,
            pl.BlockSpec((rows, EXTRA), lambda i: (0, jnp.maximum(i - first, 0))),
            pl.BlockSpec((depth, EXTRA), lambda i: (0, 0)),
        ],
        out_specs=pl.BlockSpec((depth, EXTRA), lambda i: (0, i)),
        scratch_shapes=[pltpu.VMEM((depth, rows), BF)],
        compiler_params=pltpu.CompilerParams(vmem_limit_bytes=32 << 20),
    )(normed, dpx, branch, mixed, vec)


def swap(value, axis, mask):
    count = lax.axis_size(axis)
    return lax.ppermute(value, axis, [(i, i ^ mask) for i in range(count)])


def put(buffer, piece, index, axis):
    return lax.dynamic_update_slice_in_dim(buffer, jnp.expand_dims(piece, axis), index, axis)


def take(buffer, index, axis):
    return lax.dynamic_index_in_dim(buffer, index, axis, keepdims=False)


def bits_of(axis):
    count = lax.axis_size(axis)
    assert count & (count - 1) == 0
    masks = []
    mask = count // 2
    while mask:
        masks.append(mask)
        mask //= 2
    return masks


def near_pieces(value, axis):
    stack = value[None]
    order = [0]
    for mask in bits_of(axis):
        stack = jnp.concatenate([stack, swap(stack, axis, mask)], 0)
        order = order + [m ^ mask for m in order]
    return [stack[order.index(m)] for m in range(lax.axis_size(axis))]


def ordered(pieces, axis):
    me = lax.axis_index(axis)
    out = jnp.zeros((len(pieces),) + pieces[0].shape, pieces[0].dtype)
    for m, piece in enumerate(pieces):
        out = put(out, piece, me ^ m, 0)
    return out


def gather_rows(value, axis):
    out = ordered(near_pieces(value, axis), axis)
    return out.reshape((-1,) + value.shape[1:])


def reduce_rows(value, axis):
    me = lax.axis_index(axis)
    part = value
    for mask in reversed(bits_of(axis)):
        pairs = part.reshape((-1, 2) + value.shape[1:])
        bit = (me // mask) % 2
        away = swap(take(pairs, 1 - bit, 1).astype(BF), axis, mask)
        part = take(pairs, bit, 1).astype(F32) + away.astype(F32)
    return part[0]


def trade(value, axis):
    me = lax.axis_index(axis)
    count = value.shape[0]
    held = value[:, None]
    for mask in bits_of(axis):
        halves = held.reshape((2, held.shape[0] // 2) + held.shape[1:])
        bit = (me // mask) % 2
        mine, away = take(halves, bit, 0), take(halves, 1 - bit, 0)
        got = swap(away, axis, mask)
        held = jnp.concatenate([mine, got], 1)
    held = held[0]
    out = jnp.zeros_like(held)
    masks = bits_of(axis)
    order = [0]
    for mask in masks:
        order = order + [m ^ mask for m in order]
    for at, m in enumerate(order):
        out = put(out, held[at], me ^ m, 0)
    return out


def gather_far(value, axis):
    count = lax.axis_size(axis)
    k, r, w = value.shape
    if count > 8 or count < 4 or r % 32:
        return lax.all_gather(value, axis, axis=1, tiled=True)
    me = lax.axis_index(axis)
    far, near = me // 2, me % 2
    half = r // 2
    first, second = value[:, :half], value[:, half:]
    out = jnp.zeros((k, count // 2, 2, 2, half, w), value.dtype)

    def place(out, piece, f, n, h):
        piece = piece.reshape((k, piece.size // (k * half * w), 1, 1, half, w)) if piece.ndim == 4 else piece[:, None, None, None]
        return lax.dynamic_update_slice(out, piece, (0, f, n, h, 0, 0))

    column = jnp.zeros((k, count // 2, half, w), value.dtype)
    column = put(column, first, far, 1)
    other = swap(second, axis, 1)
    pair = put(put(jnp.zeros((k, 2, half, w), value.dtype), second, near, 1), other, 1 - near, 1)
    for m in range(1, count // 2):
        column = put(column, swap(first, axis, 2 * m), far ^ m, 1)
    beside = swap(column, axis, 1)
    zero = jnp.zeros_like(far)
    out = lax.dynamic_update_slice(out, column[:, :, None, None], (zero, zero, near, zero, zero, zero))
    out = lax.dynamic_update_slice(out, beside[:, :, None, None], (zero, zero, 1 - near, zero, zero, zero))
    one = zero + 1
    out = lax.dynamic_update_slice(out, pair[:, None, :, None], (zero, far, zero, one, zero, zero))
    for m in range(1, count // 2):
        got = swap(pair, axis, 2 * m)
        out = lax.dynamic_update_slice(out, got[:, None, :, None], (zero, far ^ m, zero, one, zero, zero))
    return out.reshape(k, count * r, w)


def reduce_far(value, axis):
    count = lax.axis_size(axis)
    k, rows, w = value.shape
    r = rows // count
    if count > 8 or count < 4 or r % 32:
        return lax.psum_scatter(value, axis, scatter_dimension=1, tiled=True).astype(F32)
    me = lax.axis_index(axis)
    far, near = me // 2, me % 2
    half = r // 2
    blocks = value.reshape(k, count // 2, 2, 2, half, w)
    first, second = blocks[:, :, :, 0], blocks[:, :, :, 1]
    got = swap(take(first, 1 - near, 2), axis, 1)
    column = take(first, near, 2).astype(F32) + got.astype(F32)
    pair = take(second, far, 1).astype(F32)
    for m in range(1, count // 2):
        pair = pair + swap(take(second, far ^ m, 1), axis, 2 * m).astype(F32)
    sent = column.astype(BF)
    total_a = take(column, far, 1)
    for m in range(1, count // 2):
        total_a = total_a + swap(take(sent, far ^ m, 1), axis, 2 * m).astype(F32)
    back = swap(take(pair, 1 - near, 1).astype(BF), axis, 1)
    total_b = take(pair, near, 1) + back.astype(F32)
    return jnp.concatenate([total_a, total_b], axis=1)


def sum_everywhere(value, axes):
    for axis in axes:
        count = lax.axis_size(axis)
        if count & (count - 1):
            value = lax.psum(value, axis)
            continue
        for mask in bits_of(axis):
            value = value + swap(value, axis, mask)
    return value


def doc_positions(lengths, count):
    ends = jnp.cumsum(lengths, axis=-1)
    starts = ends - lengths
    places = jnp.arange(count, dtype=jnp.int32)
    owner = jnp.max(jnp.where(starts[None, :] <= places[:, None], starts[None, :], 0), axis=-1)
    return places - owner


def adamw(weights, moment, square, grads):
    new_moment = beta_one * moment + (1.0 - beta_one) * grads
    new_square = beta_two * square + (1.0 - beta_two) * grads * grads
    corrected = new_moment / (1.0 - beta_one**STEP)
    scaled = new_square / (1.0 - beta_two**STEP)
    new_weights = weights - learn_rate * (
        corrected / (jnp.sqrt(scaled) + adam_eps) + weight_decay * weights
    )
    return (new_weights, new_moment, new_square)


def dot(a, b, lhs=1, rhs=0):
    return lax.dot_general(a, b, (((lhs,), (rhs,)), ((), ())), preferred_element_type=F32)


def lines_of(flat, rows, half):
    size = flat.shape[-1]
    lead = flat.shape[:-1]
    per = half if size <= rows * half and size % half == 0 else size // rows
    assert size % per == 0 and size // per <= rows and per <= half
    out = flat.reshape(lead + (size // per, per))
    edge = [(0, 0)] * len(lead) + [(0, rows - size // per), (0, half - per)]
    return jnp.pad(out, edge)


def flat_of(block, size):
    rows, half = block.shape[-2:]
    per = half if size <= rows * half and size % half == 0 else size // rows
    return block[:, : size // per, :per].reshape(-1)


def local(
    activations, cotangent, live_slots, doc_lengths,
    inproj, mom_inproj, sqr_inproj,
    gateproj, mom_gateproj, sqr_gateproj,
    outproj, mom_outproj, sqr_outproj,
    mlp_gate, mom_mlp_gate, sqr_mlp_gate,
    mlp_up, mom_mlp_up, sqr_mlp_up,
    mlp_down, mom_mlp_down, sqr_mlp_down,
    vectors, mom_vectors, sqr_vectors,
    headvec, mom_headvec, sqr_headvec,
):
    n_ctx = lax.axis_size("ctx")
    me = lax.axis_index("ctx")
    assert n_ctx == H and activations.shape[0] == 1
    length = activations.shape[1]
    rows = inproj.shape[0]
    ff = mlp_gate.shape[1] // n_ctx
    half = EXTRA // 2
    live = live_slots[0].astype(F32)
    act_own, cot_own = activations[0], cotangent[0]

    in_b = inproj.astype(BF)
    gp_b = gateproj.astype(BF)
    vec_b = lines_of(vectors, rows, half).astype(BF)
    pad_b = jnp.zeros((rows, half - 2), BF)
    kq, vq, gq = H * DK, 2 * H * DK, 2 * H * DK + H * DV

    def in_slice(c):
        return jnp.concatenate(
            [
                in_b[:, c * DK : (c + 1) * DK],
                in_b[:, kq + c * DK : kq + (c + 1) * DK],
                in_b[:, vq + c * DV : vq + (c + 1) * DV],
                in_b[:, gq + c * DV : gq + (c + 1) * DV],
                gp_b[:, c : c + 1],
                gp_b[:, H + c : H + c + 1],
                pad_b,
                vec_b,
            ],
            axis=1,
        )

    out_t = outproj.T.astype(BF)
    w_one = jnp.stack(
        [jnp.concatenate([in_slice(c), out_t[:, c * DV : (c + 1) * DV]], axis=1) for c in range(n_ctx)]
    )
    w_one = trade(w_one, "ctx").reshape(1, n_ctx * rows, -1)
    full_one = gather_far(w_one, "dp")[0]
    full_in, full_out = full_one[:, : HEADG + EXTRA], full_one[:, HEADG + EXTRA :]
    tokens = jnp.concatenate([act_own, cot_own], axis=1)
    tokens = gather_rows(tokens, "ctx")
    x_full, cot_full = tokens[:, :D], tokens[:, D:]
    ff_pad = -(-ff // 256) * 256
    fill = jnp.zeros((rows, ff_pad - ff), BF)
    down_t = mlp_down.T
    w_mlp = jnp.stack(
        [
            jnp.concatenate(
                sum(([w[:, c * ff : (c + 1) * ff].astype(BF), fill] for w in (mlp_gate, mlp_up, down_t)), []),
                axis=1,
            )
            for c in range(n_ctx)
        ]
    )
    w_mlp = trade(w_mlp, "ctx").reshape(n_ctx * rows, 3 * ff_pad)
    full_mlp = lax.all_gather(w_mlp, "dp", axis=0, tiled=True)
    full_wg, full_wu, full_wd = (full_mlp[:, k * ff_pad : (k + 1) * ff_pad] for k in range(3))
    outs_near = near_pieces(full_out, "ctx")

    share = vectors.shape[0]
    vec_float = flat_of(full_in[:, HEADG + half :].astype(F32).reshape(-1, rows, half), share)
    norm_gain = vec_float[:D]
    taps_all = vec_float[D : D + CONV * CONVC].reshape(CONV, CONVC)
    mlp_gain = vec_float[D + CONV * CONVC :]
    head_gain = headvec[:DV]

    def my_taps(first, size):
        return lax.dynamic_slice_in_dim(taps_all, first + me * size, size, 1)

    taps = jnp.concatenate([my_taps(0, DK), my_taps(kq, DK), my_taps(vq, DV)], axis=1)
    par = jnp.stack(
        [
            lax.dynamic_index_in_dim(headvec, DV + me, 0, keepdims=False),
            lax.dynamic_index_in_dim(headvec, DV + H + me, 0, keepdims=False),
        ]
    )
    total = n_ctx * length
    pos = doc_positions(doc_lengths[0], total)[:, None]

    xf = x_full.astype(F32)
    inv_rms = lax.rsqrt(jnp.mean(xf * xf, -1, keepdims=True) + NORM_EPS)
    unit = xf * inv_rms
    normed = (unit * norm_gain).astype(BF)
    px = dot(normed, full_in)
    mixed, *saved = core_fwd(px, taps, par, pos, head_gain[None, :])
    branch = 0.0
    for piece, weight in zip(near_pieces(mixed, "ctx"), outs_near):
        branch = branch + dot(piece, weight, 1, 1)
    resid = xf + live * branch
    inv_two = lax.rsqrt(jnp.mean(resid * resid, -1, keepdims=True) + NORM_EPS)
    unit_two = resid * inv_two
    normed_two = (unit_two * mlp_gain).astype(BF)

    hgate = dot(normed_two, full_wg)
    hup = dot(normed_two, full_wu)
    sigma = jax.nn.sigmoid(hgate)
    silu_gate = hgate * sigma
    hidden = (silu_gate * hup).astype(BF)
    g_mlp = (cot_full.astype(F32) * live).astype(BF)
    d_hidden = dot(g_mlp, full_wd)
    d_hgate = (d_hidden * hup * sigma * (1.0 + hgate * (1.0 - sigma))).astype(BF)
    d_hup = (d_hidden * silu_gate).astype(BF)
    d_two = dot(d_hgate, full_wg, 1, 1) + dot(d_hup, full_wu, 1, 1)
    d_gain_two = jnp.sum(d_two * unit_two, axis=0)
    low, high = me % 2, me // 2
    grid = (2, 2, length, D)
    pairs = d_two.astype(BF).reshape(grid)
    got = swap(take(pairs, 1 - low, 1), "ctx", 1)
    column = take(pairs, low, 1).astype(F32) + got.astype(F32)
    d_two_col = column + swap(column.astype(BF), "ctx", 2).astype(F32)
    resid_col = take(resid.reshape(grid), low, 1)
    cot_col = take(cot_full.reshape(grid), low, 1).astype(F32)
    inv_col = lax.rsqrt(jnp.mean(resid_col * resid_col, -1, keepdims=True) + NORM_EPS)
    unit_col = resid_col * inv_col
    d_unit_two = d_two_col * mlp_gain
    d_resid_col = cot_col + inv_col * (
        d_unit_two - unit_col * jnp.mean(d_unit_two * unit_col, -1, keepdims=True)
    )
    g_col = (d_resid_col * live).astype(BF)
    g_other = swap(g_col, "ctx", 1)
    g_branch = put(put(jnp.zeros(grid, BF), g_col, low, 1), g_other, 1 - low, 1)
    g_branch = g_branch.reshape(-1, D)
    d_resid = take(d_resid_col, high, 0)
    resid_own = take(resid_col, high, 0)
    x_own = act_own.astype(F32)

    grad_mlp = mlp_grad(normed_two, g_mlp, d_hgate, d_hup, hidden)
    mlp_part = dot(hidden, full_wd, 1, 1).astype(BF)
    mlp_part, g_branch = lax.optimization_barrier((mlp_part, g_branch))
    mlp_own = reduce_rows(mlp_part.reshape(n_ctx, length, D), "ctx")
    block_out = (resid_own + live * mlp_own).astype(BF)

    d_mixed = dot(g_branch, full_out)
    d_px, d_taps, d_hgain, d_par = core_bwd(px, taps, par, pos, head_gain[None, :], d_mixed, saved)
    d_normed = dot(d_px, full_in, 1, 1)
    d_gain = jnp.sum(d_normed * unit, axis=0)
    d_taps_all = jnp.zeros((CONV, CONVC), F32)
    for piece, first, size in (
        (d_taps[:, :DK], 0, DK),
        (d_taps[:, DK : 2 * DK], kq, DK),
        (d_taps[:, 2 * DK :], vq, DV),
    ):
        d_taps_all = lax.dynamic_update_slice(d_taps_all, piece, (0, first + me * size))
    grad_vec = jnp.concatenate([d_gain, d_taps_all.reshape(-1), d_gain_two]).reshape(-1, share)
    grad_vec = jnp.pad(lines_of(grad_vec, rows, half), ((0, 0), (0, 0), (half, 0)))
    grad_one = mix_grad(normed, d_px, g_branch, mixed, grad_vec.reshape(-1, EXTRA))

    def to_owner(part):
        return trade(part.reshape(n_ctx, rows, -1).astype(BF), "ctx").astype(F32)

    own_mlp = to_owner(lax.psum_scatter(grad_mlp, "dp", scatter_dimension=0, tiled=True))
    own_one = to_owner(reduce_far(grad_one[None], "dp")[0])
    own_in, own_out = own_one[:, :, : HEADG + EXTRA], own_one[:, :, HEADG + EXTRA :]

    def beside(value, first, size):
        return [value[c, :, first : first + size] for c in range(n_ctx)]

    owned_in = jnp.concatenate(
        beside(own_in, 0, DK) + beside(own_in, DK, DK) + beside(own_in, 2 * DK, DV) + beside(own_in, HEADC, DV),
        axis=1,
    )
    owned_ab = jnp.concatenate(beside(own_in, HEADG, 1) + beside(own_in, HEADG + 1, 1), axis=1)
    owned_vec = flat_of(jnp.sum(own_in[:, :, HEADG + half :], axis=0)[None], share)
    owned_out = jnp.concatenate(beside(own_out, 0, DV), axis=1).T
    owned_wg, owned_wu, owned_wd_t = (
        jnp.concatenate(beside(own_mlp, k * ff_pad, ff), axis=1) for k in range(3)
    )
    owned_wd = owned_wd_t.T
    at_head = jnp.arange(H) == me
    grad_small = jnp.concatenate(
        [d_hgain[0], jnp.where(at_head, d_par[0, 0], 0.0), jnp.where(at_head, d_par[0, 1], 0.0)]
    )
    summed_small = sum_everywhere(grad_small, ("ctx", "dp"))

    d_normed_own = reduce_rows(d_normed.astype(BF).reshape(n_ctx, length, D), "ctx")
    inv_x = lax.rsqrt(jnp.mean(x_own * x_own, -1, keepdims=True) + NORM_EPS)
    unit_x = x_own * inv_x
    d_unit = d_normed_own * norm_gain
    input_grad = (
        d_resid + inv_x * (d_unit - unit_x * jnp.mean(d_unit * unit_x, -1, keepdims=True))
    ).astype(BF)

    n_in, nm_in, ns_in = adamw(inproj, mom_inproj, sqr_inproj, owned_in)
    n_ab, nm_ab, ns_ab = adamw(gateproj, mom_gateproj, sqr_gateproj, owned_ab)
    n_out, nm_out, ns_out = adamw(outproj, mom_outproj, sqr_outproj, owned_out)
    n_wg, nm_wg, ns_wg = adamw(mlp_gate, mom_mlp_gate, sqr_mlp_gate, owned_wg)
    n_wu, nm_wu, ns_wu = adamw(mlp_up, mom_mlp_up, sqr_mlp_up, owned_wu)
    n_wd, nm_wd, ns_wd = adamw(mlp_down, mom_mlp_down, sqr_mlp_down, owned_wd)
    n_vec, nm_vec, ns_vec = adamw(vectors, mom_vectors, sqr_vectors, owned_vec)
    n_small, nm_small, ns_small = adamw(headvec, mom_headvec, sqr_headvec, summed_small)
    return (
        block_out[None], input_grad[None],
        owned_in, owned_ab, owned_out, owned_wg, owned_wu, owned_wd, owned_vec, summed_small,
        n_in, nm_in, ns_in,
        n_ab, nm_ab, ns_ab,
        n_out, nm_out, ns_out,
        n_wg, nm_wg, ns_wg,
        n_wu, nm_wu, ns_wu,
        n_wd, nm_wd, ns_wd,
        n_vec, nm_vec, ns_vec,
        n_small, nm_small, ns_small,
    )


def solution(mesh):
    rows = P(("dp", "ctx"), None)
    cols = P(None, ("dp", "ctx"))
    flat = P(("dp", "ctx"))
    tokens = P("dp", "ctx", None)
    params = (rows,) * 6 + (cols,) * 3 + (rows,) * 6 + (cols,) * 3 + (flat,) * 3 + (P(),) * 3
    grads = (rows, rows, cols, rows, rows, cols, flat, P())
    return jax.shard_map(
        local,
        mesh=mesh,
        in_specs=(tokens, tokens, P("dp"), P("dp", None)) + params,
        out_specs=(tokens, tokens) + grads + params,
        check_vma=False,
    )
```

```python
import jax
import jax.numpy as jnp
from jax import lax
from jax.experimental import pallas as pl
from jax.experimental.pallas import tpu as pltpu
from jax.sharding import PartitionSpec as P

D = 1024
H = 4
DK = 128
DV = 256
CONV = 4
GROUP = 64
STEP = 5
CONVC = 2048

NORM_EPS = 1e-06
beta_one = 0.9
beta_two = 0.999
learn_rate = 0.01
weight_decay = 0.1
adam_eps = 1e-08

F32 = jnp.float32
BF = jnp.bfloat16
EXACT = lax.Precision.HIGHEST

HEADQ = DK
HEADC = 2 * DK + DV
HEADG = HEADC + DV
EXTRA = 128


def mm(a, b, lhs=1, rhs=0):
    return lax.dot_general(
        a, b, (((lhs,), (rhs,)), ((), ())), precision=EXACT, preferred_element_type=F32
    )


def shift_rows(value, steps):
    return pltpu.roll(value, steps % value.shape[0], axis=0)


def pre_stage(px_ref, taps_ref, par_ref, pos_ref):
    rows = px_ref.shape[0]
    pos = pos_ref[...]
    x = px_ref[:, :HEADC]
    conv = x * taps_ref[CONV - 1 : CONV, :]
    for s in range(1, CONV):
        valid = (pos >= s).astype(F32)
        conv = conv + taps_ref[CONV - 1 - s : CONV - s, :] * (shift_rows(x, s) * valid)
    sig = jax.nn.sigmoid(conv)
    act = conv * sig
    qr = act[:, :DK]
    kr = act[:, DK : 2 * DK]
    v = act[:, 2 * DK :]
    rq = lax.rsqrt(jnp.sum(qr * qr, -1, keepdims=True) + NORM_EPS)
    rk = lax.rsqrt(jnp.sum(kr * kr, -1, keepdims=True) + NORM_EPS)
    q = qr * rq * DK ** (-0.5)
    k = kr * rk
    mix = px_ref[:, HEADG : HEADG + EXTRA]
    lane = lax.broadcasted_iota(jnp.int32, (rows, EXTRA), 1)
    b_raw = jnp.sum(jnp.where(lane == 0, mix, 0.0), -1, keepdims=True)
    a_raw = jnp.sum(jnp.where(lane == 1, mix, 0.0), -1, keepdims=True)
    beta = jax.nn.sigmoid(b_raw)
    scale = -jnp.exp(jnp.zeros((rows, 1), F32) + par_ref[0])
    shifted = a_raw + par_ref[1]
    soft = jnp.maximum(shifted, 0.0) + jnp.log1p(jnp.exp(-jnp.abs(shifted)))
    logd = scale * soft
    return pos, x, conv, sig, qr, kr, rq, rk, q, k, v, beta, scale, shifted, logd


def block_masks(width):
    row = lax.broadcasted_iota(jnp.int32, (width, width), 0)
    col = lax.broadcasted_iota(jnp.int32, (width, width), 1)
    same = (row // GROUP) == (col // GROUP)
    return row, col, same


def gates_of(pos, logd, width):
    row, col, same = block_masks(width)
    lower = ((row >= col) & same).astype(F32)
    lb = jnp.broadcast_to(logd, (width, width))
    cum_t = mm(lower, lb)
    cum_i = mm(lb, lower, 0, 1)
    keep = ((row >= col) & same & (pos >= row - col)).astype(F32)
    decays = jnp.exp(jnp.minimum(cum_t - cum_i, 0.0)) * keep
    at = lax.broadcasted_iota(jnp.int32, (width, 1), 0) % GROUP
    carried = jnp.exp(cum_t[:, :1]) * (pos >= at + 1).astype(F32)
    strict = (row > col).astype(F32)
    return decays, carried, lower, strict


def unit_inverse(low):
    width = low.shape[0]
    row, col, same = block_masks(width)
    size = 1
    out = None
    while size < GROUP:
        join = (
            ((row // (2 * size)) == (col // (2 * size)))
            & ((row // size) % 2 == 1)
            & ((col // size) % 2 == 0)
        )
        part = jnp.where(join, low, 0.0)
        if out is None:
            out = (row == col).astype(F32) - part
        else:
            out = out - mm(mm(out, part), out)
        size *= 2
    return out


def final_of(decays, width):
    row, col, same = block_masks(width)
    last = ((col % GROUP) == GROUP - 1) & same
    pick = jnp.where((row % GROUP) == GROUP - 1, decays, 0.0)
    ones = jnp.ones((width, DK), F32)
    return mm(pick, ones, 0, 0)


def core_fwd_kernel(
    px_ref, taps_ref, par_ref, pos_ref, hg_ref,
    mixed_ref, state_ref, inv_ref, wr_ref, y_ref, qt_ref, m_ref, o_ref,
    n_ref,
):
    rows = px_ref.shape[0]
    width = min(4 * GROUP, rows)
    pos, x, conv, sig, qr, kr, rq, rk, q, k, v, beta, scale, shifted, logd = pre_stage(
        px_ref, taps_ref, par_ref, pos_ref
    )
    spans = [slice(i, i + width) for i in range(0, rows, width)]
    eye = (
        lax.broadcasted_iota(jnp.int32, (DK, DK), 0) == lax.broadcasted_iota(jnp.int32, (DK, DK), 1)
    ).astype(F32)
    us, pus = [], []
    for at in spans:
        decays, carried, lower, strict = gates_of(pos[at], logd[at], width)
        key_dots = mm(k[at], k[at], 1, 1)
        inv = unit_inverse(beta[at] * decays * key_dots * strict)
        inv_ref[at, :] = inv
        u = mm(inv, beta[at] * v[at])
        y = mm(inv, (beta[at] * carried) * k[at])
        p = decays * mm(q[at], k[at], 1, 1)
        qt = carried * q[at] - mm(p, y)
        pus.append(mm(p, u))
        us.append(u)
        y_ref[at, :] = y
        qt_ref[at, :] = qt
        kf = final_of(decays, width) * k[at]
        for j in range(width // GROUP):
            g = slice(j * GROUP, (j + 1) * GROUP)
            index = at.start // GROUP + j
            end = carried[(j + 1) * GROUP - 1 : (j + 1) * GROUP, :]
            m_ref[index] = end * eye - mm(kf[g], y[g], 0, 0)
            n_ref[index] = mm(kf[g], u[g], 0, 0)
    state = jnp.zeros((DK, DV), F32)
    for index in range(rows // GROUP):
        state_ref[index] = state
        if index + 1 < rows // GROUP:
            state = mm(m_ref[index], state) + n_ref[index]
    for index in range(rows // GROUP):
        g = slice(index * GROUP, (index + 1) * GROUP)
        inner = slice((index * GROUP) % width, (index * GROUP) % width + GROUP)
        state = state_ref[index]
        wr_ref[g, :] = us[index * GROUP // width][inner] - mm(y_ref[g, :], state)
        o_ref[g, :] = mm(qt_ref[g, :], state) + pus[index * GROUP // width][inner]
    out = o_ref[...]
    ro = lax.rsqrt(jnp.mean(out * out, -1, keepdims=True) + NORM_EPS)
    gate = px_ref[:, HEADC:HEADG]
    mixed_ref[...] = (out * ro * hg_ref[...] * (gate * jax.nn.sigmoid(gate))).astype(BF)


def core_bwd_kernel(
    px_ref, taps_ref, par_ref, pos_ref, hg_ref, dm_ref,
    state_ref, inv_ref, wr_ref, y_ref, qt_ref, m_ref, o_ref,
    dpx_ref, dtaps_ref, dhg_ref, dpar_ref,
    dst_ref, do_ref, dq_ref, dk_ref, dv_ref, db_ref, dg_ref,
):
    rows = px_ref.shape[0]
    width = min(4 * GROUP, rows)
    groups = rows // GROUP
    out = o_ref[...]
    ro = lax.rsqrt(jnp.mean(out * out, -1, keepdims=True) + NORM_EPS)
    on = out * ro
    gate = px_ref[:, HEADC:HEADG]
    sg = jax.nn.sigmoid(gate)
    dm = dm_ref[...]
    dpx_ref[:, HEADC:HEADG] = (dm * on * hg_ref[...] * (sg * (1.0 + gate * (1.0 - sg)))).astype(BF)
    dgained = dm * (gate * sg)
    dhg_ref[...] = jnp.sum(dgained * on, 0, keepdims=True)
    don = dgained * hg_ref[...]
    do_ref[...] = ro * (don - on * jnp.mean(don * on, -1, keepdims=True))

    pos, x, conv, sig, qr, kr, rq, rk, q, k, v, beta, scale, shifted, logd = pre_stage(
        px_ref, taps_ref, par_ref, pos_ref
    )
    back = jnp.zeros((DK, DV), F32)
    for index in reversed(range(groups)):
        g = slice(index * GROUP, (index + 1) * GROUP)
        dst_ref[index] = back
        if index:
            back = mm(m_ref[index], back, 0, 0) + mm(qt_ref[g, :], do_ref[g, :], 0, 0)
    for start in range(0, rows, width):
        at = slice(start, start + width)
        decays, carried, lower, strict = gates_of(pos[at], logd[at], width)
        qs, ks, vs, bs = q[at], k[at], v[at], beta[at]
        key_dots = mm(ks, ks, 1, 1)
        query_dots = mm(qs, ks, 1, 1)
        final = final_of(decays, width)
        kf = final * ks
        do = do_ref[at, :]
        w = wr_ref[at, :]
        inv = inv_ref[at, :]
        parts_w, parts_os, parts_kf, lasts = [], [], [], []
        for j in range(width // GROUP):
            g = slice(j * GROUP, (j + 1) * GROUP)
            index = start // GROUP + j
            parts_w.append(mm(kf[g], dst_ref[index]))
            parts_os.append(mm(do[g], state_ref[index], 1, 1))
            parts_kf.append(mm(w[g], dst_ref[index], 1, 1))
            lasts.append(
                jnp.sum(jnp.sum(dst_ref[index] * state_ref[index], -1, keepdims=True), 0, keepdims=True)
            )
        dw = mm(decays * query_dots, do, 0, 0) + jnp.concatenate(parts_w, 0)
        dtar = mm(inv, dw, 0, 0)
        dts = jnp.concatenate(
            [
                mm(dtar[j * GROUP : (j + 1) * GROUP], state_ref[start // GROUP + j], 1, 1)
                for j in range(width // GROUP)
            ],
            0,
        )
        dos = jnp.concatenate(parts_os, 0)
        dkf = jnp.concatenate(parts_kf, 0)
        dp = mm(do, w, 1, 1)
        dlow = -mm(dtar, w, 1, 1) * strict
        dqk = decays * dp
        low_dots = decays * key_dots * dlow
        dkk = bs * decays * dlow
        dq_ref[at, :] = mm(dqk, ks) + carried * dos
        k_dts = jnp.sum(ks * dts, -1, keepdims=True)
        dk_ref[at, :] = (
            mm(dqk, qs, 0, 0)
            + mm(dkk, ks)
            + mm(dkk, ks, 0, 0)
            - (bs * carried) * dts
            + final * dkf
        )
        dv_ref[at, :] = bs * dtar
        db_ref[at, :] = (
            jnp.sum(dtar * vs, -1, keepdims=True)
            - carried * k_dts
            + jnp.sum(low_dots, -1, keepdims=True)
        )
        dfinal = jnp.sum(dkf * ks, -1, keepdims=True)
        dcar = jnp.sum(qs * dos, -1, keepdims=True) - bs * k_dts
        pair = query_dots * dqk + bs * low_dots
        ones = jnp.ones((width, DK), F32)
        row_at = lax.broadcasted_iota(jnp.int32, (width, 1), 0)
        fin = dfinal * final[:, :1]
        dcum = (
            jnp.broadcast_to(jnp.sum(pair, -1, keepdims=True) + dcar * carried - fin, (width, DK))
            - mm(pair, ones, 0, 0)
        )
        for j in range(width // GROUP):
            g = slice(j * GROUP, (j + 1) * GROUP)
            e = (j + 1) * GROUP - 1
            gain = lasts[j] * carried[e : e + 1, :] + jnp.sum(fin[g], 0, keepdims=True)
            dcum = dcum + jnp.where(row_at == e, gain, 0.0)
        dg_ref[at, :] = mm(lower, dcum, 0, 0)[:, :1]

    dqn = dq_ref[...] * DK ** (-0.5)
    dkn = dk_ref[...]
    dqr = rq * (dqn - qr * (rq * rq) * jnp.sum(dqn * qr, -1, keepdims=True))
    dkr = rk * (dkn - kr * (rk * rk) * jnp.sum(dkn * kr, -1, keepdims=True))
    dact = jnp.concatenate([dqr, dkr, dv_ref[...]], -1)
    dconv = dact * (sig * (1.0 + conv * (1.0 - sig)))
    dx = dconv * taps_ref[CONV - 1 : CONV, :]
    dtaps_ref[CONV - 1 : CONV, :] = jnp.sum(dconv * x, 0, keepdims=True)
    for s in range(1, CONV):
        used = dconv * (pos >= s).astype(F32)
        dx = dx + taps_ref[CONV - 1 - s : CONV - s, :] * shift_rows(used, -s)
        dtaps_ref[CONV - 1 - s : CONV - s, :] = jnp.sum(used * shift_rows(x, s), 0, keepdims=True)
    dpx_ref[:, :HEADC] = dx.astype(BF)
    db = db_ref[...] * beta * (1.0 - beta)
    dg = dg_ref[...]
    da = dg * scale * jax.nn.sigmoid(shifted)
    lane = lax.broadcasted_iota(jnp.int32, (rows, EXTRA), 1)
    dpx_ref[:, HEADG:] = jnp.where(lane == 0, db, jnp.where(lane == 1, da, 0.0)).astype(BF)
    one = lax.broadcasted_iota(jnp.int32, (1, EXTRA), 1)
    dpar_ref[...] = jnp.where(
        one == 0,
        jnp.sum(dg * logd, 0, keepdims=True),
        jnp.where(one == 1, jnp.sum(da, 0, keepdims=True), 0.0),
    )


def vspec():
    return pl.BlockSpec(memory_space=pltpu.VMEM)


def core_fwd(px, taps, par, pos, gain):
    rows = px.shape[0]
    groups = rows // GROUP
    width = min(4 * GROUP, rows)
    shape = jax.ShapeDtypeStruct
    return pl.pallas_call(
        core_fwd_kernel,
        name="core_fwd",
        out_shape=(
            shape((rows, DV), BF),
            shape((groups, DK, DV), F32),
            shape((rows, width), F32),
            shape((rows, DV), F32),
            shape((rows, DK), F32),
            shape((rows, DK), F32),
            shape((groups, DK, DK), F32),
            shape((rows, DV), F32),
        ),
        in_specs=[vspec(), vspec(), pl.BlockSpec(memory_space=pltpu.SMEM), vspec(), vspec()],
        out_specs=tuple(vspec() for _ in range(8)),
        scratch_shapes=[pltpu.VMEM((groups, DK, DV), F32)],
        compiler_params=pltpu.CompilerParams(vmem_limit_bytes=48 << 20),
    )(px, taps, par, pos, gain)


def core_bwd(px, taps, par, pos, gain, dm, saved):
    rows = px.shape[0]
    groups = rows // GROUP
    shape = jax.ShapeDtypeStruct
    return pl.pallas_call(
        core_bwd_kernel,
        name="core_bwd",
        out_shape=(
            shape((rows, HEADG + EXTRA), BF),
            shape((CONV, HEADC), F32),
            shape((1, DV), F32),
            shape((1, EXTRA), F32),
        ),
        in_specs=[vspec(), vspec(), pl.BlockSpec(memory_space=pltpu.SMEM)]
        + [vspec() for _ in range(3 + len(saved))],
        out_specs=tuple(vspec() for _ in range(4)),
        scratch_shapes=[
            pltpu.VMEM((groups, DK, DV), F32),
            pltpu.VMEM((rows, DV), F32),
            pltpu.VMEM((rows, DK), F32),
            pltpu.VMEM((rows, DK), F32),
            pltpu.VMEM((rows, DV), F32),
            pltpu.VMEM((rows, 1), F32),
            pltpu.VMEM((rows, 1), F32),
        ],
        compiler_params=pltpu.CompilerParams(vmem_limit_bytes=48 << 20),
    )(px, taps, par, pos, gain, dm, *saved)


TILE = 256


def mlp_grad_kernel(two_ref, cot_ref, dg_ref, du_ref, hid_ref, out_ref, turned_ref):
    step = pl.program_id(0)
    third = pl.num_programs(0) // 3

    @pl.when(step == 0)
    def _():
        turned_ref[...] = two_ref[...].T

    @pl.when(step == 2 * third)
    def _():
        turned_ref[...] = cot_ref[...].T

    right = jnp.where(step < third, dg_ref[...], jnp.where(step < 2 * third, du_ref[...], hid_ref[...]))
    out_ref[...] = lax.dot_general(
        turned_ref[...], right, (((1,), (0,)), ((), ())), preferred_element_type=F32
    ).astype(BF)


def mlp_grad(two, cot, dg, du, hid):
    rows, width = dg.shape
    depth = two.shape[1]
    third = width // TILE
    whole = pl.BlockSpec((rows, depth), lambda i: (0, 0))

    def tile(first):
        return pl.BlockSpec((rows, TILE), lambda i: (0, jnp.clip(i - first, 0, third - 1)))

    return pl.pallas_call(
        mlp_grad_kernel,
        name="mlp_grad",
        grid=(3 * third,),
        out_shape=jax.ShapeDtypeStruct((depth, 3 * width), BF),
        in_specs=[whole, whole, tile(0), tile(third), tile(2 * third)],
        out_specs=pl.BlockSpec((depth, TILE), lambda i: (0, i)),
        scratch_shapes=[pltpu.VMEM((depth, rows), BF)],
        compiler_params=pltpu.CompilerParams(vmem_limit_bytes=32 << 20),
    )(two, cot, dg, du, hid)


def mix_grad_kernel(norm_ref, dpx_ref, branch_ref, mixed_ref, vec_ref, out_ref, turned_ref):
    step = pl.program_id(0)
    first = (HEADG + EXTRA) // EXTRA

    @pl.when(step == 0)
    def _():
        turned_ref[...] = norm_ref[...].T

    @pl.when(step == first)
    def _():
        turned_ref[...] = branch_ref[...].T

    right = jnp.where(step < first, dpx_ref[...], mixed_ref[...])
    got = lax.dot_general(
        turned_ref[...], right, (((1,), (0,)), ((), ())), preferred_element_type=F32
    )
    out_ref[...] = got.astype(BF)

    @pl.when(step == first - 1)
    def _():
        lane = lax.broadcasted_iota(jnp.int32, got.shape, 1)
        out_ref[...] = jnp.where(lane < EXTRA // 2, got, vec_ref[...]).astype(BF)


def mix_grad(normed, dpx, branch, mixed, vec):
    rows, depth = normed.shape
    first = dpx.shape[1] // EXTRA
    steps = first + mixed.shape[1] // EXTRA
    whole = pl.BlockSpec((rows, depth), lambda i: (0, 0))
    return pl.pallas_call(
        mix_grad_kernel,
        name="mix_grad",
        grid=(steps,),
        out_shape=jax.ShapeDtypeStruct((depth, steps * EXTRA), BF),
        in_specs=[
            whole,
            pl.BlockSpec((rows, EXTRA), lambda i: (0, jnp.minimum(i, first - 1))),
            whole,
            pl.BlockSpec((rows, EXTRA), lambda i: (0, jnp.maximum(i - first, 0))),
            pl.BlockSpec((depth, EXTRA), lambda i: (0, 0)),
        ],
        out_specs=pl.BlockSpec((depth, EXTRA), lambda i: (0, i)),
        scratch_shapes=[pltpu.VMEM((depth, rows), BF)],
        compiler_params=pltpu.CompilerParams(vmem_limit_bytes=32 << 20),
    )(normed, dpx, branch, mixed, vec)


def swap(value, axis, mask):
    count = lax.axis_size(axis)
    return lax.ppermute(value, axis, [(i, i ^ mask) for i in range(count)])


def put(buffer, piece, index, axis):
    return lax.dynamic_update_slice_in_dim(buffer, jnp.expand_dims(piece, axis), index, axis)


def take(buffer, index, axis):
    return lax.dynamic_index_in_dim(buffer, index, axis, keepdims=False)


def bits_of(axis):
    count = lax.axis_size(axis)
    assert count & (count - 1) == 0
    masks = []
    mask = count // 2
    while mask:
        masks.append(mask)
        mask //= 2
    return masks


def near_pieces(value, axis):
    stack = value[None]
    order = [0]
    for mask in bits_of(axis):
        stack = jnp.concatenate([stack, swap(stack, axis, mask)], 0)
        order = order + [m ^ mask for m in order]
    return [stack[order.index(m)] for m in range(lax.axis_size(axis))]


def ordered(pieces, axis):
    me = lax.axis_index(axis)
    out = jnp.zeros((len(pieces),) + pieces[0].shape, pieces[0].dtype)
    for m, piece in enumerate(pieces):
        out = put(out, piece, me ^ m, 0)
    return out


def gather_rows(value, axis):
    out = ordered(near_pieces(value, axis), axis)
    return out.reshape((-1,) + value.shape[1:])


def reduce_rows(value, axis):
    me = lax.axis_index(axis)
    part = value
    for mask in reversed(bits_of(axis)):
        pairs = part.reshape((-1, 2) + value.shape[1:])
        bit = (me // mask) % 2
        away = swap(take(pairs, 1 - bit, 1).astype(BF), axis, mask)
        part = take(pairs, bit, 1).astype(F32) + away.astype(F32)
    return part[0]


def trade(value, axis):
    me = lax.axis_index(axis)
    count = value.shape[0]
    held = value[:, None]
    for mask in bits_of(axis):
        halves = held.reshape((2, held.shape[0] // 2) + held.shape[1:])
        bit = (me // mask) % 2
        mine, away = take(halves, bit, 0), take(halves, 1 - bit, 0)
        got = swap(away, axis, mask)
        held = jnp.concatenate([mine, got], 1)
    held = held[0]
    out = jnp.zeros_like(held)
    masks = bits_of(axis)
    order = [0]
    for mask in masks:
        order = order + [m ^ mask for m in order]
    for at, m in enumerate(order):
        out = put(out, held[at], me ^ m, 0)
    return out


def gather_far(value, axis):
    count = lax.axis_size(axis)
    k, r, w = value.shape
    if count > 8 or count < 4 or r % 32:
        return lax.all_gather(value, axis, axis=1, tiled=True)
    me = lax.axis_index(axis)
    far, near = me // 2, me % 2
    half = r // 2
    first, second = value[:, :half], value[:, half:]
    out = jnp.zeros((k, count // 2, 2, 2, half, w), value.dtype)

    def place(out, piece, f, n, h):
        piece = piece.reshape((k, piece.size // (k * half * w), 1, 1, half, w)) if piece.ndim == 4 else piece[:, None, None, None]
        return lax.dynamic_update_slice(out, piece, (0, f, n, h, 0, 0))

    column = jnp.zeros((k, count // 2, half, w), value.dtype)
    column = put(column, first, far, 1)
    other = swap(second, axis, 1)
    pair = put(put(jnp.zeros((k, 2, half, w), value.dtype), second, near, 1), other, 1 - near, 1)
    for m in range(1, count // 2):
        column = put(column, swap(first, axis, 2 * m), far ^ m, 1)
    beside = swap(column, axis, 1)
    zero = jnp.zeros_like(far)
    out = lax.dynamic_update_slice(out, column[:, :, None, None], (zero, zero, near, zero, zero, zero))
    out = lax.dynamic_update_slice(out, beside[:, :, None, None], (zero, zero, 1 - near, zero, zero, zero))
    one = zero + 1
    out = lax.dynamic_update_slice(out, pair[:, None, :, None], (zero, far, zero, one, zero, zero))
    for m in range(1, count // 2):
        got = swap(pair, axis, 2 * m)
        out = lax.dynamic_update_slice(out, got[:, None, :, None], (zero, far ^ m, zero, one, zero, zero))
    return out.reshape(k, count * r, w)


def reduce_far(value, axis):
    count = lax.axis_size(axis)
    k, rows, w = value.shape
    r = rows // count
    if count > 8 or count < 4 or r % 32:
        return lax.psum_scatter(value, axis, scatter_dimension=1, tiled=True).astype(F32)
    me = lax.axis_index(axis)
    far, near = me // 2, me % 2
    half = r // 2
    blocks = value.reshape(k, count // 2, 2, 2, half, w)
    first, second = blocks[:, :, :, 0], blocks[:, :, :, 1]
    got = swap(take(first, 1 - near, 2), axis, 1)
    column = take(first, near, 2).astype(F32) + got.astype(F32)
    pair = take(second, far, 1).astype(F32)
    for m in range(1, count // 2):
        pair = pair + swap(take(second, far ^ m, 1), axis, 2 * m).astype(F32)
    sent = column.astype(BF)
    total_a = take(column, far, 1)
    for m in range(1, count // 2):
        total_a = total_a + swap(take(sent, far ^ m, 1), axis, 2 * m).astype(F32)
    back = swap(take(pair, 1 - near, 1).astype(BF), axis, 1)
    total_b = take(pair, near, 1) + back.astype(F32)
    return jnp.concatenate([total_a, total_b], axis=1)


def sum_everywhere(value, axes):
    for axis in axes:
        count = lax.axis_size(axis)
        if count & (count - 1):
            value = lax.psum(value, axis)
            continue
        for mask in bits_of(axis):
            value = value + swap(value, axis, mask)
    return value


def doc_positions(lengths, count):
    ends = jnp.cumsum(lengths, axis=-1)
    starts = ends - lengths
    places = jnp.arange(count, dtype=jnp.int32)
    owner = jnp.max(jnp.where(starts[None, :] <= places[:, None], starts[None, :], 0), axis=-1)
    return places - owner


def adamw(weights, moment, square, grads):
    new_moment = beta_one * moment + (1.0 - beta_one) * grads
    new_square = beta_two * square + (1.0 - beta_two) * grads * grads
    corrected = new_moment / (1.0 - beta_one**STEP)
    scaled = new_square / (1.0 - beta_two**STEP)
    new_weights = weights - learn_rate * (
        corrected / (jnp.sqrt(scaled) + adam_eps) + weight_decay * weights
    )
    return (new_weights, new_moment, new_square)


def dot(a, b, lhs=1, rhs=0):
    return lax.dot_general(a, b, (((lhs,), (rhs,)), ((), ())), preferred_element_type=F32)


def lines_of(flat, rows, half):
    size = flat.shape[-1]
    lead = flat.shape[:-1]
    per = half if size <= rows * half and size % half == 0 else size // rows
    assert size % per == 0 and size // per <= rows and per <= half
    out = flat.reshape(lead + (size // per, per))
    edge = [(0, 0)] * len(lead) + [(0, rows - size // per), (0, half - per)]
    return jnp.pad(out, edge)


def flat_of(block, size):
    rows, half = block.shape[-2:]
    per = half if size <= rows * half and size % half == 0 else size // rows
    return block[:, : size // per, :per].reshape(-1)


def local(
    activations, cotangent, live_slots, doc_lengths,
    inproj, mom_inproj, sqr_inproj,
    gateproj, mom_gateproj, sqr_gateproj,
    outproj, mom_outproj, sqr_outproj,
    mlp_gate, mom_mlp_gate, sqr_mlp_gate,
    mlp_up, mom_mlp_up, sqr_mlp_up,
    mlp_down, mom_mlp_down, sqr_mlp_down,
    vectors, mom_vectors, sqr_vectors,
    headvec, mom_headvec, sqr_headvec,
):
    n_ctx = lax.axis_size("ctx")
    me = lax.axis_index("ctx")
    assert n_ctx == H and activations.shape[0] == 1
    length = activations.shape[1]
    rows = inproj.shape[0]
    ff = mlp_gate.shape[1] // n_ctx
    half = EXTRA // 2
    live = live_slots[0].astype(F32)
    act_own, cot_own = activations[0], cotangent[0]

    in_b = inproj.astype(BF)
    gp_b = gateproj.astype(BF)
    vec_b = lines_of(vectors, rows, half).astype(BF)
    pad_b = jnp.zeros((rows, half - 2), BF)
    kq, vq, gq = H * DK, 2 * H * DK, 2 * H * DK + H * DV

    def in_slice(c):
        return jnp.concatenate(
            [
                in_b[:, c * DK : (c + 1) * DK],
                in_b[:, kq + c * DK : kq + (c + 1) * DK],
                in_b[:, vq + c * DV : vq + (c + 1) * DV],
                in_b[:, gq + c * DV : gq + (c + 1) * DV],
                gp_b[:, c : c + 1],
                gp_b[:, H + c : H + c + 1],
                pad_b,
                vec_b,
            ],
            axis=1,
        )

    out_t = outproj.T.astype(BF)
    w_one = jnp.stack(
        [jnp.concatenate([in_slice(c), out_t[:, c * DV : (c + 1) * DV]], axis=1) for c in range(n_ctx)]
    )
    w_one = trade(w_one, "ctx").reshape(1, n_ctx * rows, -1)
    ff_pad = -(-ff // 256) * 256
    fill = jnp.zeros((rows, ff_pad - ff), BF)
    down_t = mlp_down.T
    w_mlp = jnp.stack(
        [
            jnp.concatenate(
                sum(([w[:, c * ff : (c + 1) * ff].astype(BF), fill] for w in (mlp_gate, mlp_up, down_t)), []),
                axis=1,
            )
            for c in range(n_ctx)
        ]
    )
    w_mlp = trade(w_mlp, "ctx").reshape(n_ctx * rows, 3 * ff_pad)
    tokens = jnp.concatenate([act_own, cot_own], axis=1)
    w_mlp, w_one, tokens = lax.optimization_barrier((w_mlp, w_one, tokens))
    tokens = gather_rows(tokens, "ctx")
    x_full, cot_full = tokens[:, :D], tokens[:, D:]
    full_mlp = lax.all_gather(w_mlp, "dp", axis=0, tiled=True)
    full_one = gather_far(w_one, "dp")[0]
    full_in, full_out = full_one[:, : HEADG + EXTRA], full_one[:, HEADG + EXTRA :]
    full_wg, full_wu, full_wd = (full_mlp[:, k * ff_pad : (k + 1) * ff_pad] for k in range(3))

    share = vectors.shape[0]
    vec_float = flat_of(full_in[:, HEADG + half :].astype(F32).reshape(-1, rows, half), share)
    norm_gain = vec_float[:D]
    taps_all = vec_float[D : D + CONV * CONVC].reshape(CONV, CONVC)
    mlp_gain = vec_float[D + CONV * CONVC :]
    head_gain = headvec[:DV]

    def my_taps(first, size):
        return lax.dynamic_slice_in_dim(taps_all, first + me * size, size, 1)

    taps = jnp.concatenate([my_taps(0, DK), my_taps(kq, DK), my_taps(vq, DV)], axis=1)
    par = jnp.stack(
        [
            lax.dynamic_index_in_dim(headvec, DV + me, 0, keepdims=False),
            lax.dynamic_index_in_dim(headvec, DV + H + me, 0, keepdims=False),
        ]
    )
    total = n_ctx * length
    pos = doc_positions(doc_lengths[0], total)[:, None]

    xf = x_full.astype(F32)
    inv_rms = lax.rsqrt(jnp.mean(xf * xf, -1, keepdims=True) + NORM_EPS)
    unit = xf * inv_rms
    normed = (unit * norm_gain).astype(BF)
    px = dot(normed, full_in)
    px, out_away = lax.optimization_barrier((px, full_out))
    outs_near = near_pieces(out_away, "ctx")
    mixed, *saved = core_fwd(px, taps, par, pos, head_gain[None, :])
    branch = 0.0
    for piece, weight in zip(near_pieces(mixed, "ctx"), outs_near):
        branch = branch + dot(piece, weight, 1, 1)
    resid = xf + live * branch
    inv_two = lax.rsqrt(jnp.mean(resid * resid, -1, keepdims=True) + NORM_EPS)
    unit_two = resid * inv_two
    normed_two = (unit_two * mlp_gain).astype(BF)

    hgate = dot(normed_two, full_wg)
    hup = dot(normed_two, full_wu)
    sigma = jax.nn.sigmoid(hgate)
    silu_gate = hgate * sigma
    hidden = (silu_gate * hup).astype(BF)
    g_mlp = (cot_full.astype(F32) * live).astype(BF)
    d_hidden = dot(g_mlp, full_wd)
    d_hgate = (d_hidden * hup * sigma * (1.0 + hgate * (1.0 - sigma))).astype(BF)
    d_hup = (d_hidden * silu_gate).astype(BF)
    d_two = dot(d_hgate, full_wg, 1, 1) + dot(d_hup, full_wu, 1, 1)
    d_gain_two = jnp.sum(d_two * unit_two, axis=0)
    low, high = me % 2, me // 2
    grid = (2, 2, length, D)
    pairs = d_two.astype(BF).reshape(grid)
    got = swap(take(pairs, 1 - low, 1), "ctx", 1)
    column = take(pairs, low, 1).astype(F32) + got.astype(F32)
    grad_mlp = mlp_grad(normed_two, g_mlp, d_hgate, d_hup, hidden)
    met, _ = lax.optimization_barrier((swap(column.astype(BF), "ctx", 2), grad_mlp))
    d_two_col = column + met.astype(F32)
    resid_col = take(resid.reshape(grid), low, 1)
    cot_col = take(cot_full.reshape(grid), low, 1).astype(F32)
    inv_col = lax.rsqrt(jnp.mean(resid_col * resid_col, -1, keepdims=True) + NORM_EPS)
    unit_col = resid_col * inv_col
    d_unit_two = d_two_col * mlp_gain
    d_resid_col = cot_col + inv_col * (
        d_unit_two - unit_col * jnp.mean(d_unit_two * unit_col, -1, keepdims=True)
    )
    g_col = (d_resid_col * live).astype(BF)
    g_other = swap(g_col, "ctx", 1)
    g_branch = put(put(jnp.zeros(grid, BF), g_col, low, 1), g_other, 1 - low, 1)
    g_branch = g_branch.reshape(-1, D)
    d_resid = take(d_resid_col, high, 0)
    resid_own = take(resid_col, high, 0)
    x_own = act_own.astype(F32)

    mlp_part = dot(hidden, full_wd, 1, 1).astype(BF)
    mlp_part, g_branch = lax.optimization_barrier((mlp_part, g_branch))
    mlp_own = reduce_rows(mlp_part.reshape(n_ctx, length, D), "ctx")
    block_out = (resid_own + live * mlp_own).astype(BF)

    d_mixed = dot(g_branch, full_out)
    d_px, d_taps, d_hgain, d_par = core_bwd(px, taps, par, pos, head_gain[None, :], d_mixed, saved)
    d_normed = dot(d_px, full_in, 1, 1)
    d_gain = jnp.sum(d_normed * unit, axis=0)
    d_taps_all = jnp.zeros((CONV, CONVC), F32)
    for piece, first, size in (
        (d_taps[:, :DK], 0, DK),
        (d_taps[:, DK : 2 * DK], kq, DK),
        (d_taps[:, 2 * DK :], vq, DV),
    ):
        d_taps_all = lax.dynamic_update_slice(d_taps_all, piece, (0, first + me * size))
    grad_vec = jnp.concatenate([d_gain, d_taps_all.reshape(-1), d_gain_two]).reshape(-1, share)
    grad_vec = jnp.pad(lines_of(grad_vec, rows, half), ((0, 0), (0, 0), (half, 0)))
    grad_one = mix_grad(normed, d_px, g_branch, mixed, grad_vec.reshape(-1, EXTRA))

    def to_owner(part):
        return trade(part.reshape(n_ctx, rows, -1).astype(BF), "ctx").astype(F32)

    own_mlp = to_owner(lax.psum_scatter(grad_mlp, "dp", scatter_dimension=0, tiled=True))
    far_one, d_normed_b = lax.optimization_barrier(
        (reduce_far(grad_one[None], "dp")[0], d_normed.astype(BF))
    )
    own_one = to_owner(far_one)
    own_in, own_out = own_one[:, :, : HEADG + EXTRA], own_one[:, :, HEADG + EXTRA :]
    at_head = jnp.arange(H) == me
    grad_small = jnp.concatenate(
        [d_hgain[0], jnp.where(at_head, d_par[0, 0], 0.0), jnp.where(at_head, d_par[0, 1], 0.0)]
    )
    grad_small, own_one = lax.optimization_barrier((grad_small, own_one))
    own_in, own_out = own_one[:, :, : HEADG + EXTRA], own_one[:, :, HEADG + EXTRA :]
    summed_small = sum_everywhere(grad_small, ("ctx", "dp"))


    def beside(value, first, size):
        return [value[c, :, first : first + size] for c in range(n_ctx)]

    owned_in = jnp.concatenate(
        beside(own_in, 0, DK) + beside(own_in, DK, DK) + beside(own_in, 2 * DK, DV) + beside(own_in, HEADC, DV),
        axis=1,
    )
    owned_ab = jnp.concatenate(beside(own_in, HEADG, 1) + beside(own_in, HEADG + 1, 1), axis=1)
    owned_vec = flat_of(jnp.sum(own_in[:, :, HEADG + half :], axis=0)[None], share)
    owned_out = jnp.concatenate(beside(own_out, 0, DV), axis=1).T
    owned_wg, owned_wu, owned_wd_t = (
        jnp.concatenate(beside(own_mlp, k * ff_pad, ff), axis=1) for k in range(3)
    )
    owned_wd = owned_wd_t.T
    d_normed_own = reduce_rows(d_normed_b.reshape(n_ctx, length, D), "ctx")
    inv_x = lax.rsqrt(jnp.mean(x_own * x_own, -1, keepdims=True) + NORM_EPS)
    unit_x = x_own * inv_x
    d_unit = d_normed_own * norm_gain
    input_grad = (
        d_resid + inv_x * (d_unit - unit_x * jnp.mean(d_unit * unit_x, -1, keepdims=True))
    ).astype(BF)

    n_in, nm_in, ns_in = adamw(inproj, mom_inproj, sqr_inproj, owned_in)
    n_ab, nm_ab, ns_ab = adamw(gateproj, mom_gateproj, sqr_gateproj, owned_ab)
    n_out, nm_out, ns_out = adamw(outproj, mom_outproj, sqr_outproj, owned_out)
    n_wg, nm_wg, ns_wg = adamw(mlp_gate, mom_mlp_gate, sqr_mlp_gate, owned_wg)
    n_wu, nm_wu, ns_wu = adamw(mlp_up, mom_mlp_up, sqr_mlp_up, owned_wu)
    n_wd, nm_wd, ns_wd = adamw(mlp_down, mom_mlp_down, sqr_mlp_down, owned_wd)
    n_vec, nm_vec, ns_vec = adamw(vectors, mom_vectors, sqr_vectors, owned_vec)
    n_small, nm_small, ns_small = adamw(headvec, mom_headvec, sqr_headvec, summed_small)
    return (
        block_out[None], input_grad[None],
        owned_in, owned_ab, owned_out, owned_wg, owned_wu, owned_wd, owned_vec, summed_small,
        n_in, nm_in, ns_in,
        n_ab, nm_ab, ns_ab,
        n_out, nm_out, ns_out,
        n_wg, nm_wg, ns_wg,
        n_wu, nm_wu, ns_wu,
        n_wd, nm_wd, ns_wd,
        n_vec, nm_vec, ns_vec,
        n_small, nm_small, ns_small,
    )


def solution(mesh):
    rows = P(("dp", "ctx"), None)
    cols = P(None, ("dp", "ctx"))
    flat = P(("dp", "ctx"))
    tokens = P("dp", "ctx", None)
    params = (rows,) * 6 + (cols,) * 3 + (rows,) * 6 + (cols,) * 3 + (flat,) * 3 + (P(),) * 3
    grads = (rows, rows, cols, rows, rows, cols, flat, P())
    return jax.shard_map(
        local,
        mesh=mesh,
        in_specs=(tokens, tokens, P("dp"), P("dp", None)) + params,
        out_specs=(tokens, tokens) + grads + params,
        check_vma=False,
    )
```

```python
import jax
import jax.numpy as jnp
from jax import lax
from jax.experimental import pallas as pl
from jax.experimental.pallas import tpu as pltpu
from jax.sharding import PartitionSpec as P

D = 1024
H = 4
DK = 128
DV = 256
CONV = 4
GROUP = 64
STEP = 5
CONVC = 2048

NORM_EPS = 1e-06
beta_one = 0.9
beta_two = 0.999
learn_rate = 0.01
weight_decay = 0.1
adam_eps = 1e-08

F32 = jnp.float32
BF = jnp.bfloat16
EXACT = lax.Precision.HIGHEST

HEADQ = DK
HEADC = 2 * DK + DV
HEADG = HEADC + DV
EXTRA = 128


def mm(a, b, lhs=1, rhs=0):
    return lax.dot_general(
        a, b, (((lhs,), (rhs,)), ((), ())), precision=EXACT, preferred_element_type=F32
    )


def shift_rows(value, steps):
    return pltpu.roll(value, steps % value.shape[0], axis=0)


def pre_stage(px_ref, taps_ref, par_ref, pos_ref):
    rows = px_ref.shape[0]
    pos = pos_ref[...]
    x = px_ref[:, :HEADC]
    conv = x * taps_ref[CONV - 1 : CONV, :]
    for s in range(1, CONV):
        valid = (pos >= s).astype(F32)
        conv = conv + taps_ref[CONV - 1 - s : CONV - s, :] * (shift_rows(x, s) * valid)
    sig = jax.nn.sigmoid(conv)
    act = conv * sig
    qr = act[:, :DK]
    kr = act[:, DK : 2 * DK]
    v = act[:, 2 * DK :]
    rq = lax.rsqrt(jnp.sum(qr * qr, -1, keepdims=True) + NORM_EPS)
    rk = lax.rsqrt(jnp.sum(kr * kr, -1, keepdims=True) + NORM_EPS)
    q = qr * rq * DK ** (-0.5)
    k = kr * rk
    mix = px_ref[:, HEADG : HEADG + EXTRA]
    lane = lax.broadcasted_iota(jnp.int32, (rows, EXTRA), 1)
    b_raw = jnp.sum(jnp.where(lane == 0, mix, 0.0), -1, keepdims=True)
    a_raw = jnp.sum(jnp.where(lane == 1, mix, 0.0), -1, keepdims=True)
    beta = jax.nn.sigmoid(b_raw)
    scale = -jnp.exp(jnp.zeros((rows, 1), F32) + par_ref[0])
    shifted = a_raw + par_ref[1]
    soft = jnp.maximum(shifted, 0.0) + jnp.log1p(jnp.exp(-jnp.abs(shifted)))
    logd = scale * soft
    return pos, x, conv, sig, qr, kr, rq, rk, q, k, v, beta, scale, shifted, logd


def block_masks(width):
    row = lax.broadcasted_iota(jnp.int32, (width, width), 0)
    col = lax.broadcasted_iota(jnp.int32, (width, width), 1)
    same = (row // GROUP) == (col // GROUP)
    return row, col, same


def gates_of(pos, logd, width):
    row, col, same = block_masks(width)
    lower = ((row >= col) & same).astype(F32)
    lb = jnp.broadcast_to(logd, (width, width))
    cum_t = mm(lower, lb)
    cum_i = mm(lb, lower, 0, 1)
    keep = ((row >= col) & same & (pos >= row - col)).astype(F32)
    decays = jnp.exp(jnp.minimum(cum_t - cum_i, 0.0)) * keep
    at = lax.broadcasted_iota(jnp.int32, (width, 1), 0) % GROUP
    carried = jnp.exp(cum_t[:, :1]) * (pos >= at + 1).astype(F32)
    strict = (row > col).astype(F32)
    return decays, carried, lower, strict


def unit_inverse(low):
    width = low.shape[0]
    row, col, same = block_masks(width)
    size = 1
    out = None
    while size < GROUP:
        join = (
            ((row // (2 * size)) == (col // (2 * size)))
            & ((row // size) % 2 == 1)
            & ((col // size) % 2 == 0)
        )
        part = jnp.where(join, low, 0.0)
        if out is None:
            out = (row == col).astype(F32) - part
        else:
            out = out - mm(mm(out, part), out)
        size *= 2
    return out


def final_of(decays, width):
    row, col, same = block_masks(width)
    last = ((col % GROUP) == GROUP - 1) & same
    pick = jnp.where((row % GROUP) == GROUP - 1, decays, 0.0)
    ones = jnp.ones((width, DK), F32)
    return mm(pick, ones, 0, 0)


def core_fwd_kernel(
    px_ref, taps_ref, par_ref, pos_ref, hg_ref,
    mixed_ref, state_ref, inv_ref, wr_ref, y_ref, qt_ref, m_ref, o_ref,
    n_ref,
):
    rows = px_ref.shape[0]
    width = min(4 * GROUP, rows)
    pos, x, conv, sig, qr, kr, rq, rk, q, k, v, beta, scale, shifted, logd = pre_stage(
        px_ref, taps_ref, par_ref, pos_ref
    )
    spans = [slice(i, i + width) for i in range(0, rows, width)]
    eye = (
        lax.broadcasted_iota(jnp.int32, (DK, DK), 0) == lax.broadcasted_iota(jnp.int32, (DK, DK), 1)
    ).astype(F32)
    us, pus = [], []
    for at in spans:
        decays, carried, lower, strict = gates_of(pos[at], logd[at], width)
        key_dots = mm(k[at], k[at], 1, 1)
        inv = unit_inverse(beta[at] * decays * key_dots * strict)
        inv_ref[at, :] = inv
        u = mm(inv, beta[at] * v[at])
        y = mm(inv, (beta[at] * carried) * k[at])
        p = decays * mm(q[at], k[at], 1, 1)
        qt = carried * q[at] - mm(p, y)
        pus.append(mm(p, u))
        us.append(u)
        y_ref[at, :] = y
        qt_ref[at, :] = qt
        kf = final_of(decays, width) * k[at]
        for j in range(width // GROUP):
            g = slice(j * GROUP, (j + 1) * GROUP)
            index = at.start // GROUP + j
            end = carried[(j + 1) * GROUP - 1 : (j + 1) * GROUP, :]
            m_ref[index] = end * eye - mm(kf[g], y[g], 0, 0)
            n_ref[index] = mm(kf[g], u[g], 0, 0)
    state = jnp.zeros((DK, DV), F32)
    for index in range(rows // GROUP):
        state_ref[index] = state
        if index + 1 < rows // GROUP:
            state = mm(m_ref[index], state) + n_ref[index]
    for index in range(rows // GROUP):
        g = slice(index * GROUP, (index + 1) * GROUP)
        inner = slice((index * GROUP) % width, (index * GROUP) % width + GROUP)
        state = state_ref[index]
        wr_ref[g, :] = us[index * GROUP // width][inner] - mm(y_ref[g, :], state)
        o_ref[g, :] = mm(qt_ref[g, :], state) + pus[index * GROUP // width][inner]
    out = o_ref[...]
    ro = lax.rsqrt(jnp.mean(out * out, -1, keepdims=True) + NORM_EPS)
    gate = px_ref[:, HEADC:HEADG]
    mixed_ref[...] = (out * ro * hg_ref[...] * (gate * jax.nn.sigmoid(gate))).astype(BF)


def core_bwd_kernel(
    px_ref, taps_ref, par_ref, pos_ref, hg_ref, dm_ref,
    state_ref, inv_ref, wr_ref, y_ref, qt_ref, m_ref, o_ref,
    dpx_ref, dtaps_ref, dhg_ref, dpar_ref,
    dst_ref, do_ref, dq_ref, dk_ref, dv_ref, db_ref, dg_ref,
):
    rows = px_ref.shape[0]
    width = min(4 * GROUP, rows)
    groups = rows // GROUP
    out = o_ref[...]
    ro = lax.rsqrt(jnp.mean(out * out, -1, keepdims=True) + NORM_EPS)
    on = out * ro
    gate = px_ref[:, HEADC:HEADG]
    sg = jax.nn.sigmoid(gate)
    dm = dm_ref[...]
    dpx_ref[:, HEADC:HEADG] = (dm * on * hg_ref[...] * (sg * (1.0 + gate * (1.0 - sg)))).astype(BF)
    dgained = dm * (gate * sg)
    dhg_ref[...] = jnp.sum(dgained * on, 0, keepdims=True)
    don = dgained * hg_ref[...]
    do_ref[...] = ro * (don - on * jnp.mean(don * on, -1, keepdims=True))

    pos, x, conv, sig, qr, kr, rq, rk, q, k, v, beta, scale, shifted, logd = pre_stage(
        px_ref, taps_ref, par_ref, pos_ref
    )
    back = jnp.zeros((DK, DV), F32)
    for index in reversed(range(groups)):
        g = slice(index * GROUP, (index + 1) * GROUP)
        dst_ref[index] = back
        if index:
            back = mm(m_ref[index], back, 0, 0) + mm(qt_ref[g, :], do_ref[g, :], 0, 0)
    for start in range(0, rows, width):
        at = slice(start, start + width)
        decays, carried, lower, strict = gates_of(pos[at], logd[at], width)
        qs, ks, vs, bs = q[at], k[at], v[at], beta[at]
        key_dots = mm(ks, ks, 1, 1)
        query_dots = mm(qs, ks, 1, 1)
        final = final_of(decays, width)
        kf = final * ks
        do = do_ref[at, :]
        w = wr_ref[at, :]
        inv = inv_ref[at, :]
        parts_w, parts_os, parts_kf, lasts = [], [], [], []
        for j in range(width // GROUP):
            g = slice(j * GROUP, (j + 1) * GROUP)
            index = start // GROUP + j
            parts_w.append(mm(kf[g], dst_ref[index]))
            parts_os.append(mm(do[g], state_ref[index], 1, 1))
            parts_kf.append(mm(w[g], dst_ref[index], 1, 1))
            lasts.append(
                jnp.sum(jnp.sum(dst_ref[index] * state_ref[index], -1, keepdims=True), 0, keepdims=True)
            )
        dw = mm(decays * query_dots, do, 0, 0) + jnp.concatenate(parts_w, 0)
        dtar = mm(inv, dw, 0, 0)
        dts = jnp.concatenate(
            [
                mm(dtar[j * GROUP : (j + 1) * GROUP], state_ref[start // GROUP + j], 1, 1)
                for j in range(width // GROUP)
            ],
            0,
        )
        dos = jnp.concatenate(parts_os, 0)
        dkf = jnp.concatenate(parts_kf, 0)
        dp = mm(do, w, 1, 1)
        dlow = -mm(dtar, w, 1, 1) * strict
        dqk = decays * dp
        low_dots = decays * key_dots * dlow
        dkk = bs * decays * dlow
        dq_ref[at, :] = mm(dqk, ks) + carried * dos
        k_dts = jnp.sum(ks * dts, -1, keepdims=True)
        dk_ref[at, :] = (
            mm(dqk, qs, 0, 0)
            + mm(dkk, ks)
            + mm(dkk, ks, 0, 0)
            - (bs * carried) * dts
            + final * dkf
        )
        dv_ref[at, :] = bs * dtar
        db_ref[at, :] = (
            jnp.sum(dtar * vs, -1, keepdims=True)
            - carried * k_dts
            + jnp.sum(low_dots, -1, keepdims=True)
        )
        dfinal = jnp.sum(dkf * ks, -1, keepdims=True)
        dcar = jnp.sum(qs * dos, -1, keepdims=True) - bs * k_dts
        pair = query_dots * dqk + bs * low_dots
        ones = jnp.ones((width, DK), F32)
        row_at = lax.broadcasted_iota(jnp.int32, (width, 1), 0)
        fin = dfinal * final[:, :1]
        dcum = (
            jnp.broadcast_to(jnp.sum(pair, -1, keepdims=True) + dcar * carried - fin, (width, DK))
            - mm(pair, ones, 0, 0)
        )
        for j in range(width // GROUP):
            g = slice(j * GROUP, (j + 1) * GROUP)
            e = (j + 1) * GROUP - 1
            gain = lasts[j] * carried[e : e + 1, :] + jnp.sum(fin[g], 0, keepdims=True)
            dcum = dcum + jnp.where(row_at == e, gain, 0.0)
        dg_ref[at, :] = mm(lower, dcum, 0, 0)[:, :1]

    dqn = dq_ref[...] * DK ** (-0.5)
    dkn = dk_ref[...]
    dqr = rq * (dqn - qr * (rq * rq) * jnp.sum(dqn * qr, -1, keepdims=True))
    dkr = rk * (dkn - kr * (rk * rk) * jnp.sum(dkn * kr, -1, keepdims=True))
    dact = jnp.concatenate([dqr, dkr, dv_ref[...]], -1)
    dconv = dact * (sig * (1.0 + conv * (1.0 - sig)))
    dx = dconv * taps_ref[CONV - 1 : CONV, :]
    dtaps_ref[CONV - 1 : CONV, :] = jnp.sum(dconv * x, 0, keepdims=True)
    for s in range(1, CONV):
        used = dconv * (pos >= s).astype(F32)
        dx = dx + taps_ref[CONV - 1 - s : CONV - s, :] * shift_rows(used, -s)
        dtaps_ref[CONV - 1 - s : CONV - s, :] = jnp.sum(used * shift_rows(x, s), 0, keepdims=True)
    dpx_ref[:, :HEADC] = dx.astype(BF)
    db = db_ref[...] * beta * (1.0 - beta)
    dg = dg_ref[...]
    da = dg * scale * jax.nn.sigmoid(shifted)
    lane = lax.broadcasted_iota(jnp.int32, (rows, EXTRA), 1)
    dpx_ref[:, HEADG:] = jnp.where(lane == 0, db, jnp.where(lane == 1, da, 0.0)).astype(BF)
    one = lax.broadcasted_iota(jnp.int32, (1, EXTRA), 1)
    dpar_ref[...] = jnp.where(
        one == 0,
        jnp.sum(dg * logd, 0, keepdims=True),
        jnp.where(one == 1, jnp.sum(da, 0, keepdims=True), 0.0),
    )


def vspec():
    return pl.BlockSpec(memory_space=pltpu.VMEM)


def core_fwd(px, taps, par, pos, gain):
    rows = px.shape[0]
    groups = rows // GROUP
    width = min(4 * GROUP, rows)
    shape = jax.ShapeDtypeStruct
    return pl.pallas_call(
        core_fwd_kernel,
        name="core_fwd",
        out_shape=(
            shape((rows, DV), BF),
            shape((groups, DK, DV), F32),
            shape((rows, width), F32),
            shape((rows, DV), F32),
            shape((rows, DK), F32),
            shape((rows, DK), F32),
            shape((groups, DK, DK), F32),
            shape((rows, DV), F32),
        ),
        in_specs=[vspec(), vspec(), pl.BlockSpec(memory_space=pltpu.SMEM), vspec(), vspec()],
        out_specs=tuple(vspec() for _ in range(8)),
        scratch_shapes=[pltpu.VMEM((groups, DK, DV), F32)],
        compiler_params=pltpu.CompilerParams(vmem_limit_bytes=48 << 20),
    )(px, taps, par, pos, gain)


def core_bwd(px, taps, par, pos, gain, dm, saved):
    rows = px.shape[0]
    groups = rows // GROUP
    shape = jax.ShapeDtypeStruct
    return pl.pallas_call(
        core_bwd_kernel,
        name="core_bwd",
        out_shape=(
            shape((rows, HEADG + EXTRA), BF),
            shape((CONV, HEADC), F32),
            shape((1, DV), F32),
            shape((1, EXTRA), F32),
        ),
        in_specs=[vspec(), vspec(), pl.BlockSpec(memory_space=pltpu.SMEM)]
        + [vspec() for _ in range(3 + len(saved))],
        out_specs=tuple(vspec() for _ in range(4)),
        scratch_shapes=[
            pltpu.VMEM((groups, DK, DV), F32),
            pltpu.VMEM((rows, DV), F32),
            pltpu.VMEM((rows, DK), F32),
            pltpu.VMEM((rows, DK), F32),
            pltpu.VMEM((rows, DV), F32),
            pltpu.VMEM((rows, 1), F32),
            pltpu.VMEM((rows, 1), F32),
        ],
        compiler_params=pltpu.CompilerParams(vmem_limit_bytes=48 << 20),
    )(px, taps, par, pos, gain, dm, *saved)


TILE = 256


def mlp_grad_kernel(two_ref, cot_ref, dg_ref, du_ref, hid_ref, out_ref, turned_ref):
    step = pl.program_id(0)
    third = pl.num_programs(0) // 3

    @pl.when(step == 0)
    def _():
        turned_ref[...] = two_ref[...].T

    @pl.when(step == 2 * third)
    def _():
        turned_ref[...] = cot_ref[...].T

    right = jnp.where(step < third, dg_ref[...], jnp.where(step < 2 * third, du_ref[...], hid_ref[...]))
    out_ref[...] = lax.dot_general(
        turned_ref[...], right, (((1,), (0,)), ((), ())), preferred_element_type=F32
    ).astype(BF)


def mlp_grad(two, cot, dg, du, hid):
    rows, width = dg.shape
    depth = two.shape[1]
    third = width // TILE
    whole = pl.BlockSpec((rows, depth), lambda i: (0, 0))

    def tile(first):
        return pl.BlockSpec((rows, TILE), lambda i: (0, jnp.clip(i - first, 0, third - 1)))

    return pl.pallas_call(
        mlp_grad_kernel,
        name="mlp_grad",
        grid=(3 * third,),
        out_shape=jax.ShapeDtypeStruct((depth, 3 * width), BF),
        in_specs=[whole, whole, tile(0), tile(third), tile(2 * third)],
        out_specs=pl.BlockSpec((depth, TILE), lambda i: (0, i)),
        scratch_shapes=[pltpu.VMEM((depth, rows), BF)],
        compiler_params=pltpu.CompilerParams(vmem_limit_bytes=32 << 20),
    )(two, cot, dg, du, hid)


def mix_grad_kernel(norm_ref, dpx_ref, branch_ref, mixed_ref, vec_ref, out_ref, turned_ref):
    step = pl.program_id(0)
    first = (HEADG + EXTRA) // EXTRA

    @pl.when(step == 0)
    def _():
        turned_ref[...] = norm_ref[...].T

    @pl.when(step == first)
    def _():
        turned_ref[...] = branch_ref[...].T

    right = jnp.where(step < first, dpx_ref[...], mixed_ref[...])
    got = lax.dot_general(
        turned_ref[...], right, (((1,), (0,)), ((), ())), preferred_element_type=F32
    )
    out_ref[...] = got.astype(BF)

    @pl.when(step == first - 1)
    def _():
        lane = lax.broadcasted_iota(jnp.int32, got.shape, 1)
        out_ref[...] = jnp.where(lane < EXTRA // 2, got, vec_ref[...]).astype(BF)


def mix_grad(normed, dpx, branch, mixed, vec):
    rows, depth = normed.shape
    first = dpx.shape[1] // EXTRA
    steps = first + mixed.shape[1] // EXTRA
    whole = pl.BlockSpec((rows, depth), lambda i: (0, 0))
    return pl.pallas_call(
        mix_grad_kernel,
        name="mix_grad",
        grid=(steps,),
        out_shape=jax.ShapeDtypeStruct((depth, steps * EXTRA), BF),
        in_specs=[
            whole,
            pl.BlockSpec((rows, EXTRA), lambda i: (0, jnp.minimum(i, first - 1))),
            whole,
            pl.BlockSpec((rows, EXTRA), lambda i: (0, jnp.maximum(i - first, 0))),
            pl.BlockSpec((depth, EXTRA), lambda i: (0, 0)),
        ],
        out_specs=pl.BlockSpec((depth, EXTRA), lambda i: (0, i)),
        scratch_shapes=[pltpu.VMEM((depth, rows), BF)],
        compiler_params=pltpu.CompilerParams(vmem_limit_bytes=32 << 20),
    )(normed, dpx, branch, mixed, vec)


def swap(value, axis, mask):
    count = lax.axis_size(axis)
    return lax.ppermute(value, axis, [(i, i ^ mask) for i in range(count)])


def put(buffer, piece, index, axis):
    return lax.dynamic_update_slice_in_dim(buffer, jnp.expand_dims(piece, axis), index, axis)


def take(buffer, index, axis):
    return lax.dynamic_index_in_dim(buffer, index, axis, keepdims=False)


def bits_of(axis):
    count = lax.axis_size(axis)
    assert count & (count - 1) == 0
    masks = []
    mask = count // 2
    while mask:
        masks.append(mask)
        mask //= 2
    return masks


def near_pieces(value, axis):
    stack = value[None]
    order = [0]
    for mask in bits_of(axis):
        stack = jnp.concatenate([stack, swap(stack, axis, mask)], 0)
        order = order + [m ^ mask for m in order]
    return [stack[order.index(m)] for m in range(lax.axis_size(axis))]


def ordered(pieces, axis):
    me = lax.axis_index(axis)
    out = jnp.zeros((len(pieces),) + pieces[0].shape, pieces[0].dtype)
    for m, piece in enumerate(pieces):
        out = put(out, piece, me ^ m, 0)
    return out


def gather_rows(value, axis):
    out = ordered(near_pieces(value, axis), axis)
    return out.reshape((-1,) + value.shape[1:])


def reduce_rows(value, axis):
    me = lax.axis_index(axis)
    part = value
    for mask in reversed(bits_of(axis)):
        pairs = part.reshape((-1, 2) + value.shape[1:])
        bit = (me // mask) % 2
        away = swap(take(pairs, 1 - bit, 1).astype(BF), axis, mask)
        part = take(pairs, bit, 1).astype(F32) + away.astype(F32)
    return part[0]


def trade(value, axis):
    me = lax.axis_index(axis)
    count = value.shape[0]
    held = value[:, None]
    for mask in bits_of(axis):
        halves = held.reshape((2, held.shape[0] // 2) + held.shape[1:])
        bit = (me // mask) % 2
        mine, away = take(halves, bit, 0), take(halves, 1 - bit, 0)
        got = swap(away, axis, mask)
        held = jnp.concatenate([mine, got], 1)
    held = held[0]
    out = jnp.zeros_like(held)
    masks = bits_of(axis)
    order = [0]
    for mask in masks:
        order = order + [m ^ mask for m in order]
    for at, m in enumerate(order):
        out = put(out, held[at], me ^ m, 0)
    return out


def gather_far(value, axis):
    count = lax.axis_size(axis)
    k, r, w = value.shape
    if count > 8 or count < 4 or r % 32:
        return lax.all_gather(value, axis, axis=1, tiled=True)
    me = lax.axis_index(axis)
    far, near = me // 2, me % 2
    half = r // 2
    first, second = value[:, :half], value[:, half:]
    out = jnp.zeros((k, count // 2, 2, 2, half, w), value.dtype)

    def place(out, piece, f, n, h):
        piece = piece.reshape((k, piece.size // (k * half * w), 1, 1, half, w)) if piece.ndim == 4 else piece[:, None, None, None]
        return lax.dynamic_update_slice(out, piece, (0, f, n, h, 0, 0))

    column = jnp.zeros((k, count // 2, half, w), value.dtype)
    column = put(column, first, far, 1)
    other = swap(second, axis, 1)
    pair = put(put(jnp.zeros((k, 2, half, w), value.dtype), second, near, 1), other, 1 - near, 1)
    for m in range(1, count // 2):
        column = put(column, swap(first, axis, 2 * m), far ^ m, 1)
    beside = swap(column, axis, 1)
    zero = jnp.zeros_like(far)
    out = lax.dynamic_update_slice(out, column[:, :, None, None], (zero, zero, near, zero, zero, zero))
    out = lax.dynamic_update_slice(out, beside[:, :, None, None], (zero, zero, 1 - near, zero, zero, zero))
    one = zero + 1
    out = lax.dynamic_update_slice(out, pair[:, None, :, None], (zero, far, zero, one, zero, zero))
    for m in range(1, count // 2):
        got = swap(pair, axis, 2 * m)
        out = lax.dynamic_update_slice(out, got[:, None, :, None], (zero, far ^ m, zero, one, zero, zero))
    return out.reshape(k, count * r, w)


def reduce_far(value, axis):
    count = lax.axis_size(axis)
    k, rows, w = value.shape
    r = rows // count
    if count > 8 or count < 4 or r % 32:
        return lax.psum_scatter(value, axis, scatter_dimension=1, tiled=True).astype(F32)
    me = lax.axis_index(axis)
    far, near = me // 2, me % 2
    half = r // 2
    blocks = value.reshape(k, count // 2, 2, 2, half, w)
    first, second = blocks[:, :, :, 0], blocks[:, :, :, 1]
    got = swap(take(first, 1 - near, 2), axis, 1)
    column = take(first, near, 2).astype(F32) + got.astype(F32)
    pair = take(second, far, 1).astype(F32)
    for m in range(1, count // 2):
        pair = pair + swap(take(second, far ^ m, 1), axis, 2 * m).astype(F32)
    sent = column.astype(BF)
    total_a = take(column, far, 1)
    for m in range(1, count // 2):
        total_a = total_a + swap(take(sent, far ^ m, 1), axis, 2 * m).astype(F32)
    back = swap(take(pair, 1 - near, 1).astype(BF), axis, 1)
    total_b = take(pair, near, 1) + back.astype(F32)
    return jnp.concatenate([total_a, total_b], axis=1)


def sum_everywhere(value, axes):
    for axis in axes:
        count = lax.axis_size(axis)
        if count & (count - 1):
            value = lax.psum(value, axis)
            continue
        for mask in bits_of(axis):
            value = value + swap(value, axis, mask)
    return value


def doc_positions(lengths, count):
    ends = jnp.cumsum(lengths, axis=-1)
    starts = ends - lengths
    places = jnp.arange(count, dtype=jnp.int32)
    owner = jnp.max(jnp.where(starts[None, :] <= places[:, None], starts[None, :], 0), axis=-1)
    return places - owner


def adamw(weights, moment, square, grads):
    new_moment = beta_one * moment + (1.0 - beta_one) * grads
    new_square = beta_two * square + (1.0 - beta_two) * grads * grads
    corrected = new_moment / (1.0 - beta_one**STEP)
    scaled = new_square / (1.0 - beta_two**STEP)
    new_weights = weights - learn_rate * (
        corrected / (jnp.sqrt(scaled) + adam_eps) + weight_decay * weights
    )
    return (new_weights, new_moment, new_square)


def dot(a, b, lhs=1, rhs=0):
    return lax.dot_general(a, b, (((lhs,), (rhs,)), ((), ())), preferred_element_type=F32)


def lines_of(flat, rows, half):
    size = flat.shape[-1]
    lead = flat.shape[:-1]
    per = half if size <= rows * half and size % half == 0 else size // rows
    assert size % per == 0 and size // per <= rows and per <= half
    out = flat.reshape(lead + (size // per, per))
    edge = [(0, 0)] * len(lead) + [(0, rows - size // per), (0, half - per)]
    return jnp.pad(out, edge)


def flat_of(block, size):
    rows, half = block.shape[-2:]
    per = half if size <= rows * half and size % half == 0 else size // rows
    return block[:, : size // per, :per].reshape(-1)


def local(
    activations, cotangent, live_slots, doc_lengths,
    inproj, mom_inproj, sqr_inproj,
    gateproj, mom_gateproj, sqr_gateproj,
    outproj, mom_outproj, sqr_outproj,
    mlp_gate, mom_mlp_gate, sqr_mlp_gate,
    mlp_up, mom_mlp_up, sqr_mlp_up,
    mlp_down, mom_mlp_down, sqr_mlp_down,
    vectors, mom_vectors, sqr_vectors,
    headvec, mom_headvec, sqr_headvec,
):
    n_ctx = lax.axis_size("ctx")
    me = lax.axis_index("ctx")
    assert n_ctx == H and activations.shape[0] == 1
    length = activations.shape[1]
    rows = inproj.shape[0]
    ff = mlp_gate.shape[1] // n_ctx
    half = EXTRA // 2
    live = live_slots[0].astype(F32)
    act_own, cot_own = activations[0], cotangent[0]

    in_b = inproj.astype(BF)
    gp_b = gateproj.astype(BF)
    vec_b = lines_of(vectors, rows, half).astype(BF)
    pad_b = jnp.zeros((rows, half - 2), BF)
    kq, vq, gq = H * DK, 2 * H * DK, 2 * H * DK + H * DV

    def in_slice(c):
        return jnp.concatenate(
            [
                in_b[:, c * DK : (c + 1) * DK],
                in_b[:, kq + c * DK : kq + (c + 1) * DK],
                in_b[:, vq + c * DV : vq + (c + 1) * DV],
                in_b[:, gq + c * DV : gq + (c + 1) * DV],
                gp_b[:, c : c + 1],
                gp_b[:, H + c : H + c + 1],
                pad_b,
                vec_b,
            ],
            axis=1,
        )

    out_t = outproj.T.astype(BF)
    w_one = jnp.stack(
        [jnp.concatenate([in_slice(c), out_t[:, c * DV : (c + 1) * DV]], axis=1) for c in range(n_ctx)]
    )
    w_one = trade(w_one, "ctx").reshape(1, n_ctx * rows, -1)
    ff_pad = -(-ff // 256) * 256
    fill = jnp.zeros((rows, ff_pad - ff), BF)
    down_t = mlp_down.T
    w_mlp = jnp.stack(
        [
            jnp.concatenate(
                sum(([w[:, c * ff : (c + 1) * ff].astype(BF), fill] for w in (mlp_gate, mlp_up, down_t)), []),
                axis=1,
            )
            for c in range(n_ctx)
        ]
    )
    w_mlp = trade(w_mlp, "ctx").reshape(n_ctx * rows, 3 * ff_pad)
    tokens = jnp.concatenate([act_own, cot_own], axis=1)
    w_mlp, w_one, tokens = lax.optimization_barrier((w_mlp, w_one, tokens))
    tokens = gather_rows(tokens, "ctx")
    x_full, cot_full = tokens[:, :D], tokens[:, D:]
    full_mlp = lax.all_gather(w_mlp, "dp", axis=0, tiled=True)
    full_one = gather_far(w_one, "dp")[0]
    full_in, full_out = full_one[:, : HEADG + EXTRA], full_one[:, HEADG + EXTRA :]
    full_wg, full_wu, full_wd = (full_mlp[:, k * ff_pad : (k + 1) * ff_pad] for k in range(3))

    share = vectors.shape[0]
    vec_float = flat_of(full_in[:, HEADG + half :].astype(F32).reshape(-1, rows, half), share)
    norm_gain = vec_float[:D]
    taps_all = vec_float[D : D + CONV * CONVC].reshape(CONV, CONVC)
    mlp_gain = vec_float[D + CONV * CONVC :]
    head_gain = headvec[:DV]

    def my_taps(first, size):
        return lax.dynamic_slice_in_dim(taps_all, first + me * size, size, 1)

    taps = jnp.concatenate([my_taps(0, DK), my_taps(kq, DK), my_taps(vq, DV)], axis=1)
    par = jnp.stack(
        [
            lax.dynamic_index_in_dim(headvec, DV + me, 0, keepdims=False),
            lax.dynamic_index_in_dim(headvec, DV + H + me, 0, keepdims=False),
        ]
    )
    total = n_ctx * length
    pos = doc_positions(doc_lengths[0], total)[:, None]

    xf = x_full.astype(F32)
    inv_rms = lax.rsqrt(jnp.mean(xf * xf, -1, keepdims=True) + NORM_EPS)
    unit = xf * inv_rms
    normed = (unit * norm_gain).astype(BF)
    px = dot(normed, full_in)
    px, out_away = lax.optimization_barrier((px, full_out))
    out_far = swap(out_away, "ctx", 2)
    mixed, *saved = core_fwd(px, taps, par, pos, head_gain[None, :])
    mixed, out_far = lax.optimization_barrier((mixed, out_far))
    outs_near = [out_away, swap(out_away, "ctx", 1), out_far, swap(out_far, "ctx", 1)]
    branch = 0.0
    for piece, weight in zip(near_pieces(mixed, "ctx"), outs_near):
        branch = branch + dot(piece, weight, 1, 1)
    resid = xf + live * branch
    inv_two = lax.rsqrt(jnp.mean(resid * resid, -1, keepdims=True) + NORM_EPS)
    unit_two = resid * inv_two
    normed_two = (unit_two * mlp_gain).astype(BF)

    hgate = dot(normed_two, full_wg)
    hup = dot(normed_two, full_wu)
    sigma = jax.nn.sigmoid(hgate)
    silu_gate = hgate * sigma
    hidden = (silu_gate * hup).astype(BF)
    g_mlp = (cot_full.astype(F32) * live).astype(BF)
    d_hidden = dot(g_mlp, full_wd)
    d_hgate = (d_hidden * hup * sigma * (1.0 + hgate * (1.0 - sigma))).astype(BF)
    d_hup = (d_hidden * silu_gate).astype(BF)
    d_two = dot(d_hgate, full_wg, 1, 1) + dot(d_hup, full_wu, 1, 1)
    d_gain_two = jnp.sum(d_two * unit_two, axis=0)
    low, high = me % 2, me // 2
    grid = (2, 2, length, D)
    grad_mlp = mlp_grad(normed_two, g_mlp, d_hgate, d_hup, hidden)
    pairs, _ = lax.optimization_barrier((d_two.astype(BF).reshape(grid), grad_mlp))
    got = swap(take(pairs, 1 - low, 1), "ctx", 1)
    column = take(pairs, low, 1).astype(F32) + got.astype(F32)
    d_two_col = column + swap(column.astype(BF), "ctx", 2).astype(F32)
    resid_col = take(resid.reshape(grid), low, 1)
    cot_col = take(cot_full.reshape(grid), low, 1).astype(F32)
    inv_col = lax.rsqrt(jnp.mean(resid_col * resid_col, -1, keepdims=True) + NORM_EPS)
    unit_col = resid_col * inv_col
    d_unit_two = d_two_col * mlp_gain
    d_resid_col = cot_col + inv_col * (
        d_unit_two - unit_col * jnp.mean(d_unit_two * unit_col, -1, keepdims=True)
    )
    g_col = (d_resid_col * live).astype(BF)
    g_other = swap(g_col, "ctx", 1)
    g_branch = put(put(jnp.zeros(grid, BF), g_col, low, 1), g_other, 1 - low, 1)
    g_branch = g_branch.reshape(-1, D)
    d_resid = take(d_resid_col, high, 0)
    resid_own = take(resid_col, high, 0)
    x_own = act_own.astype(F32)

    mlp_part = dot(hidden, full_wd, 1, 1).astype(BF)
    mlp_part, g_branch = lax.optimization_barrier((mlp_part, g_branch))
    mlp_own = reduce_rows(mlp_part.reshape(n_ctx, length, D), "ctx")
    block_out = (resid_own + live * mlp_own).astype(BF)

    d_mixed = dot(g_branch, full_out)
    d_px, d_taps, d_hgain, d_par = core_bwd(px, taps, par, pos, head_gain[None, :], d_mixed, saved)
    d_normed = dot(d_px, full_in, 1, 1)
    d_gain = jnp.sum(d_normed * unit, axis=0)
    d_taps_all = jnp.zeros((CONV, CONVC), F32)
    for piece, first, size in (
        (d_taps[:, :DK], 0, DK),
        (d_taps[:, DK : 2 * DK], kq, DK),
        (d_taps[:, 2 * DK :], vq, DV),
    ):
        d_taps_all = lax.dynamic_update_slice(d_taps_all, piece, (0, first + me * size))
    grad_vec = jnp.concatenate([d_gain, d_taps_all.reshape(-1), d_gain_two]).reshape(-1, share)
    grad_vec = jnp.pad(lines_of(grad_vec, rows, half), ((0, 0), (0, 0), (half, 0)))
    grad_one = mix_grad(normed, d_px, g_branch, mixed, grad_vec.reshape(-1, EXTRA))

    def to_owner(part):
        return trade(part.reshape(n_ctx, rows, -1).astype(BF), "ctx").astype(F32)

    own_mlp = to_owner(lax.psum_scatter(grad_mlp, "dp", scatter_dimension=0, tiled=True))
    far_one, d_normed_b = lax.optimization_barrier(
        (reduce_far(grad_one[None], "dp")[0], d_normed.astype(BF))
    )
    own_one = to_owner(far_one)
    own_in, own_out = own_one[:, :, : HEADG + EXTRA], own_one[:, :, HEADG + EXTRA :]
    at_head = jnp.arange(H) == me
    grad_small = jnp.concatenate(
        [d_hgain[0], jnp.where(at_head, d_par[0, 0], 0.0), jnp.where(at_head, d_par[0, 1], 0.0)]
    )
    grad_small, own_one = lax.optimization_barrier((grad_small, own_one))
    own_in, own_out = own_one[:, :, : HEADG + EXTRA], own_one[:, :, HEADG + EXTRA :]
    summed_small = sum_everywhere(grad_small, ("ctx", "dp"))


    def beside(value, first, size):
        return [value[c, :, first : first + size] for c in range(n_ctx)]

    owned_in = jnp.concatenate(
        beside(own_in, 0, DK) + beside(own_in, DK, DK) + beside(own_in, 2 * DK, DV) + beside(own_in, HEADC, DV),
        axis=1,
    )
    owned_ab = jnp.concatenate(beside(own_in, HEADG, 1) + beside(own_in, HEADG + 1, 1), axis=1)
    owned_vec = flat_of(jnp.sum(own_in[:, :, HEADG + half :], axis=0)[None], share)
    owned_out = jnp.concatenate(beside(own_out, 0, DV), axis=1).T
    owned_wg, owned_wu, owned_wd_t = (
        jnp.concatenate(beside(own_mlp, k * ff_pad, ff), axis=1) for k in range(3)
    )
    owned_wd = owned_wd_t.T
    d_normed_own = reduce_rows(d_normed_b.reshape(n_ctx, length, D), "ctx")
    inv_x = lax.rsqrt(jnp.mean(x_own * x_own, -1, keepdims=True) + NORM_EPS)
    unit_x = x_own * inv_x
    d_unit = d_normed_own * norm_gain
    input_grad = (
        d_resid + inv_x * (d_unit - unit_x * jnp.mean(d_unit * unit_x, -1, keepdims=True))
    ).astype(BF)

    n_in, nm_in, ns_in = adamw(inproj, mom_inproj, sqr_inproj, owned_in)
    n_ab, nm_ab, ns_ab = adamw(gateproj, mom_gateproj, sqr_gateproj, owned_ab)
    n_out, nm_out, ns_out = adamw(outproj, mom_outproj, sqr_outproj, owned_out)
    n_wg, nm_wg, ns_wg = adamw(mlp_gate, mom_mlp_gate, sqr_mlp_gate, owned_wg)
    n_wu, nm_wu, ns_wu = adamw(mlp_up, mom_mlp_up, sqr_mlp_up, owned_wu)
    n_wd, nm_wd, ns_wd = adamw(mlp_down, mom_mlp_down, sqr_mlp_down, owned_wd)
    n_vec, nm_vec, ns_vec = adamw(vectors, mom_vectors, sqr_vectors, owned_vec)
    n_small, nm_small, ns_small = adamw(headvec, mom_headvec, sqr_headvec, summed_small)
    return (
        block_out[None], input_grad[None],
        owned_in, owned_ab, owned_out, owned_wg, owned_wu, owned_wd, owned_vec, summed_small,
        n_in, nm_in, ns_in,
        n_ab, nm_ab, ns_ab,
        n_out, nm_out, ns_out,
        n_wg, nm_wg, ns_wg,
        n_wu, nm_wu, ns_wu,
        n_wd, nm_wd, ns_wd,
        n_vec, nm_vec, ns_vec,
        n_small, nm_small, ns_small,
    )


def solution(mesh):
    rows = P(("dp", "ctx"), None)
    cols = P(None, ("dp", "ctx"))
    flat = P(("dp", "ctx"))
    tokens = P("dp", "ctx", None)
    params = (rows,) * 6 + (cols,) * 3 + (rows,) * 6 + (cols,) * 3 + (flat,) * 3 + (P(),) * 3
    grads = (rows, rows, cols, rows, rows, cols, flat, P())
    return jax.shard_map(
        local,
        mesh=mesh,
        in_specs=(tokens, tokens, P("dp"), P("dp", None)) + params,
        out_specs=(tokens, tokens) + grads + params,
        check_vma=False,
    )
```
